256 devices in a mesh: grp: 4 (over y_lo, core), trk: 64 (over z, x, y_hi).
Axes of the slice: x: 4, y: 4 (y_hi: 2, y_lo: 2; y = y_hi * 2 + y_lo), z: 8, core: 2. Of those that a mesh axis runs over, the one named last changes fastest.
Arguments:
- fields: bfloat16 [256, 512, 512], P('grp', 'trk'), may hold values from -81 to 81
- upstream: bfloat16 [256, 512, 512], P('grp', 'trk'), may hold values from -6 to 6
- ln_gain: float32 [512], replicated, may hold values from 0.1 to 1.9
- weights: bfloat16 [4, 512, 512], P(None, 'grp', 'trk'), may hold values from -8 to 8
Outputs:
- grad_fields: bfloat16 [256, 512, 512], P('grp', 'trk')
- grad_weights: float32 [4, 512, 512], P(None, 'grp', 'trk')
- grad_gain: float32 [512], replicated
The draws below stay inside these ranges and needn't reach their ends.
All inputs are finite; a program needn't handle non-finite values.
Results may differ from the reference program's by a relative error of at most 0.014.
The reference program's roundings to bfloat16 on the way count: a program that leaves them out, or rounds other values in their place, can miss the bound.
Values may be sent and summed in bfloat16 or wider, within the bound.
A program may use at most 64 MiB of HBM per device.

```python
import jax
import jax.numpy as jnp
from jax import lax

D = 512
HEADS = 8
TRACK = 512
HT = 256


def draw_fields(key, part):
    first_key = jax.random.fold_in(key, 0)
    values = jnp.clip(jax.random.normal(first_key, (HT, TRACK, D), jnp.float32), -8.0, 8.0)
    return values.astype(jnp.bfloat16)


def draw_weights(key, part):
    first_key = jax.random.fold_in(key, 0)
    values = jnp.clip(jax.random.normal(first_key, (4, D, D), jnp.float32), -6.0, 6.0) * D ** (-0.5)
    return values.astype(jnp.bfloat16)


def block_levels(stream_key, extent, cuts, least, largest):
    level = 1.0
    for axis_at, parts in cuts:
        steps = jax.random.uniform(jax.random.fold_in(jax.random.fold_in(stream_key, 6), axis_at), (parts,), jnp.float32, least / len(cuts), largest / len(cuts))
        level = level * jnp.repeat(jnp.exp(steps), extent[axis_at] // parts).reshape((-1,) + (1,) * (len(extent) - 1 - axis_at))
    return level


def scatter_about(stream_key, shape, scale, most, cuts=(), held_as=jnp.bfloat16):
    entries = jax.random.normal(stream_key, shape, jnp.float32) * scale
    if len(cuts) > 0:
        entries = block_levels(stream_key, shape, cuts, -0.22, 0.18) * entries
    return jnp.clip(entries, min=-most, max=most).astype(held_as)


def setup_inputs(seed: int = 0) -> dict:
    streams_of = jax.random.split(jax.random.key(seed), 5)
    return {
        "fields": draw_fields(jax.random.fold_in(streams_of[4], 71), 0),
        "upstream": scatter_about(streams_of[1], (HT, TRACK, D), 1.0, 6.0, ((0, 4), (1, 64))),
        "ln_gain": jnp.clip(1.0 + 0.18 * jax.random.normal(streams_of[2], (D,), jnp.float32), 0.1, 1.9),
        "weights": draw_weights(jax.random.fold_in(streams_of[4], 71), 0),
    }


def rounded(block):
    return lax.optimization_barrier(block.astype(jnp.bfloat16)).astype(jnp.float32)

def normalize(fields, ln_gain):
    values = fields.astype(jnp.float32)
    row_mean = lax.optimization_barrier(jnp.mean(values, -1, keepdims=True))
    offset = values - row_mean
    row_var = lax.optimization_barrier(jnp.mean(offset * offset, -1, keepdims=True))
    inv_std = lax.rsqrt(row_var + 1e-05)
    centred = offset * inv_std
    normed = (centred * ln_gain).astype(jnp.bfloat16)
    return (normed, centred, inv_std)

def split_heads(block):
    rows, length, width = block.shape
    return block.reshape(rows, length, HEADS, width // HEADS).transpose(0, 2, 1, 3).reshape(rows * HEADS, length, width // HEADS)

def merge_heads(block, rows):
    items, length, size = block.shape
    return block.reshape(rows, items // rows, length, size).transpose(0, 2, 1, 3).reshape(rows, length, items // rows * size)

def head_back(members):
    query, keyed, valued, grad_out = [member.astype(jnp.float32) for member in members]
    scaling = query.shape[-1] ** (-0.5)
    scores = jnp.einsum('qd,kd->qk', query, keyed) * scaling
    row_max = lax.optimization_barrier(jnp.max(scores, -1, keepdims=True))
    shifted = jnp.exp(scores - row_max)
    attn_prob = shifted / lax.optimization_barrier(jnp.sum(shifted, -1, keepdims=True))
    prob_low = rounded(attn_prob)
    output = jnp.einsum('qk,kd->qd', prob_low, valued).astype(jnp.bfloat16)
    dprobs = jnp.einsum('qd,kd->qk', grad_out, valued)
    row_dot = lax.optimization_barrier(jnp.sum(attn_prob * dprobs, -1, keepdims=True))
    score_grad = rounded(attn_prob * (dprobs - row_dot) * scaling)
    grad_value = jnp.einsum('qk,qd->kd', prob_low, grad_out).astype(jnp.bfloat16)
    grad_query = jnp.einsum('qk,kd->qd', score_grad, keyed).astype(jnp.bfloat16)
    grad_key = jnp.einsum('qk,qd->kd', score_grad, query).astype(jnp.bfloat16)
    return (output, grad_query, grad_key, grad_value)

def reference(fields, upstream, ln_gain, weights):
    rows, length, width = fields.shape
    normed, centred, inv_std = normalize(fields, ln_gain)
    flat = normed.reshape(-1, width)
    projected = [jnp.dot(flat, weights[index], preferred_element_type=jnp.float32).astype(jnp.bfloat16).reshape(rows, length, width) for index in range(3)]
    up_flat = upstream.reshape(-1, width)
    grad_attended = jnp.dot(up_flat, weights[3].T, preferred_element_type=jnp.float32).astype(jnp.bfloat16).reshape(rows, length, width)
    pieces = lax.map(head_back, (split_heads(projected[0]), split_heads(projected[1]), split_heads(projected[2]), split_heads(grad_attended)))
    attended, grad_query, grad_key, grad_value = [merge_heads(piece, rows).reshape(-1, width) for piece in pieces]
    raw_grad = jnp.stack([jnp.dot(flat.T, grad_query, preferred_element_type=jnp.float32), jnp.dot(flat.T, grad_key, preferred_element_type=jnp.float32), jnp.dot(flat.T, grad_value, preferred_element_type=jnp.float32), jnp.dot(attended.T, up_flat, preferred_element_type=jnp.float32)])
    stacked = jnp.stack([grad_query, grad_key, grad_value], 1).astype(jnp.float32)
    grad_normed = jnp.einsum('tcj,cij->ti', stacked, weights[:3].astype(jnp.float32)).reshape(rows, length, width)
    raw_gain = lax.optimization_barrier(jnp.sum((grad_normed * centred).reshape(-1, width), 0))
    scaled = grad_normed * ln_gain
    branch = inv_std * (scaled - lax.optimization_barrier(jnp.mean(scaled, -1, keepdims=True)) - centred * lax.optimization_barrier(jnp.mean(scaled * centred, -1, keepdims=True)))
    branch = branch.astype(jnp.bfloat16)
    grad_fields = (upstream.astype(jnp.float32) + branch.astype(jnp.float32)).astype(jnp.bfloat16)
    factor = float(rows * length) ** (-0.5)
    return (grad_fields, raw_grad * factor, raw_gain * factor)
```

```python
import jax
import jax.numpy as jnp
from jax import lax
from jax.experimental import pallas as pl
from jax.experimental.pallas import tpu as pltpu
from jax.sharding import PartitionSpec as P

NZ, NX, NYH = 8, 4, 2
NYL, NC = 2, 2
HEAD = 64
MESH = pl.DeviceIdType.MESH
F32, BF16 = jnp.float32, jnp.bfloat16


def dot(a, b, ca, cb):
    return lax.dot_general(a, b, (((ca,), (cb,)), ((), ())), preferred_element_type=F32)


def position():
    grp, trk = lax.axis_index("grp"), lax.axis_index("trk")
    z, x, y_hi = trk // (NX * NYH), (trk // NYH) % NX, trk % NYH
    y_lo, core = grp // NC, grp % NC
    return grp, trk, z, x, y_hi, y_lo, core


def trk_of(z, x, y_hi):
    return (z * NX + x) * NYH + y_hi


def remote(src, dst, send, recv, grp, trk):
    return pltpu.make_async_remote_copy(
        src_ref=src, dst_ref=dst, send_sem=send, recv_sem=recv,
        device_id=(grp, trk), device_id_type=MESH,
    )


def enter(grp, trk, y_hi, y_lo, core, z, x):
    tracks = NZ * NX * NYH
    barrier = pltpu.get_barrier_semaphore()

    def greet(step, carry):
        pl.semaphore_signal(
            barrier, inc=1, device_id=(grp, lax.rem(trk + step, tracks)), device_id_type=MESH
        )
        return carry

    pl.semaphore_signal(barrier, inc=1, device_id=(y_lo * NC + 1 - core, trk), device_id_type=MESH)
    for far in range(NYH):
        pl.semaphore_signal(
            barrier,
            inc=1,
            device_id=((1 - y_lo) * NC + core, trk_of(z, x, (y_hi + far) % NYH)),
            device_id_type=MESH,
        )
    lax.fori_loop(1, tracks, greet, 0)
    pl.semaphore_wait(barrier, tracks - 1 + 1 + NYH)


def exchange_start(src, dst, send, recv, local, grp, trk):
    tracks = NZ * NX * NYH

    def send_one(step, carry):
        to = lax.rem(trk + step, tracks)
        remote(src.at[to], dst.at[trk], send, recv, grp, to).start()
        return carry

    lax.fori_loop(1, tracks, send_one, 0)
    pltpu.make_async_copy(src.at[trk], dst.at[trk], local).start()


def exchange_wait(src, dst, send, recv, local, grp, trk):
    tracks = NZ * NX * NYH
    rest = pl.ds(0, tracks - 1)
    whole = remote(src.at[rest], dst.at[rest], send, recv, grp, trk)
    whole.wait_recv()
    whole.wait_send()
    pltpu.make_async_copy(src.at[trk], dst.at[trk], local).wait()


def wait_all(view, send, recv, grp, trk):
    whole = remote(view, view, send, recv, grp, trk)
    whole.wait_send()
    whole.wait_recv()


def lanes(grp):
    return pl.ds(pl.multiple_of(grp * 128, 128), 128)


def gather_kernel(f_ref, u_ref, w_ref, fr_ref, ur_ref, wf_ref, send, recv, local):
    grp, trk, z, x, y_hi, y_lo, core = position()
    enter(grp, trk, y_hi, y_lo, core, z, x)
    mine = wf_ref.at[:, z, x, y_hi, :, lanes(grp)]
    own = pltpu.make_async_copy(w_ref, mine, local.at[2])
    own.start()
    along_z = [
        remote(w_ref, mine, send.at[2], recv.at[2], grp, trk_of((z + s) % NZ, x, y_hi))
        for s in range(1, NZ)
    ]
    for copy in along_z:
        copy.start()
    exchange_start(f_ref, fr_ref, send.at[0], recv.at[0], local.at[0], grp, trk)
    own.wait()
    wait_all(wf_ref.at[:, : NZ - 1, 0, 0, :, :128], send.at[2], recv.at[2], grp, trk)
    column = wf_ref.at[:, :, x, y_hi, :, lanes(grp)]
    along_x = [
        remote(column, column, send.at[3], recv.at[3], grp, trk_of(z, (x + s) % NX, y_hi))
        for s in range(1, NX)
    ]
    for copy in along_x:
        copy.start()
    exchange_start(u_ref, ur_ref, send.at[1], recv.at[1], local.at[1], grp, trk)
    wait_all(wf_ref.at[:, :, : NX - 1, 0, :, :128], send.at[3], recv.at[3], grp, trk)
    plane = wf_ref.at[:, :, :, y_hi, :, lanes(grp)]
    along_y = [
        remote(
            plane, plane, send.at[4], recv.at[4],
            ((y_lo + s % 2) % NYL) * NC + core, trk_of(z, x, (y_hi + s // 2) % NYH),
        )
        for s in range(1, NYL * NYH)
    ]
    for copy in along_y:
        copy.start()
    wait_all(wf_ref.at[:, :, :, 0, :, : (NYL * NYH - 1) * 128], send.at[4], recv.at[4], grp, trk)
    across = []
    for low in range(NYL):
        half = wf_ref.at[:, :, :, :, :, lanes(low * NC + core)]
        across.append(remote(half, half, send.at[5], recv.at[5], y_lo * NC + 1 - core, trk))
    for copy in across:
        copy.start()
    wait_all(wf_ref.at[:, :, :, :, :, : NYL * 128], send.at[5], recv.at[5], grp, trk)
    exchange_wait(f_ref, fr_ref, send.at[0], recv.at[0], local.at[0], grp, trk)
    exchange_wait(u_ref, ur_ref, send.at[1], recv.at[1], local.at[1], grp, trk)


def gather(fields, upstream, w_tile):
    tracks, cells, width = fields.shape
    rows = jax.ShapeDtypeStruct((tracks, cells, width), BF16)
    return pl.pallas_call(
        gather_kernel,
        out_shape=(
            rows,
            rows,
            jax.ShapeDtypeStruct((4, NZ, NX, NYH, w_tile.shape[1], width), BF16),
        ),
        in_specs=[pl.BlockSpec(memory_space=pl.ANY)] * 3,
        out_specs=[pl.BlockSpec(memory_space=pl.ANY)] * 3,
        scratch_shapes=[
            pltpu.SemaphoreType.DMA((6,)),
            pltpu.SemaphoreType.DMA((6,)),
            pltpu.SemaphoreType.DMA((3,)),
        ],
        compiler_params=pltpu.CompilerParams(collective_id=1, has_side_effects=True),
        name="gather_rows",
    )(fields, upstream, w_tile)


def row_kernel(
    f_ref, u_ref, w_ref, gain_ref, gf_ref, raw_ref, gg_ref,
    cen_ref, inv_ref, nor_ref, q_ref, k_ref, v_ref, ga_ref, at_ref, gq_ref, gk_ref, gv_ref,
):
    gain = gain_ref[...]
    values = f_ref[...].astype(F32)
    row_mean = jnp.mean(values, -1, keepdims=True)
    offset = values - row_mean
    inv_std = lax.rsqrt(jnp.mean(offset * offset, -1, keepdims=True) + 1e-05)
    centred = offset * inv_std
    cen_ref[...] = centred
    inv_ref[...] = inv_std
    nor_ref[...] = (centred * gain).astype(BF16)
    scaling = HEAD ** (-0.5)
    for index, ref in enumerate((q_ref, k_ref, v_ref)):
        ref[...] = dot(nor_ref[...], w_ref[index], 1, 1).astype(BF16)
    ga_ref[...] = dot(u_ref[...], w_ref[3], 1, 0).astype(BF16)
    width = f_ref.shape[1]
    length = f_ref.shape[0]
    half = length // 2
    lane = lax.broadcasted_iota(jnp.int32, (1, 128), 1)

    def pair(index, carry):
        cols = pl.ds(pl.multiple_of(index * 128, 128), 128)
        q, k, v, ga = q_ref[:, cols], k_ref[:, cols], v_ref[:, cols], ga_ref[:, cols]
        sum_k = jnp.zeros((length, 128), F32)
        sum_v = jnp.zeros((length, 128), F32)
        for part in range(2):
            rows = slice(part * half, (part + 1) * half)
            sum_o = jnp.zeros((half, 128), F32)
            sum_q = jnp.zeros((half, 128), F32)
            for head in range(2):
                mask = ((lane >= head * HEAD) & (lane < (head + 1) * HEAD)).astype(BF16)
                k_h, v_h = k * mask, v * mask
                q_h, ga_h = q[rows] * mask, ga[rows] * mask
                scores = dot(k_h, q[rows], 1, 1) * scaling
                shifted = jnp.exp(scores - jnp.max(scores, 0, keepdims=True))
                prob = shifted * (1.0 / jnp.sum(shifted, 0, keepdims=True))
                prob_low = prob.astype(BF16)
                dprobs = dot(v_h, ga[rows], 1, 1)
                row_dot = jnp.sum(prob * dprobs, 0, keepdims=True)
                grad = (prob * (dprobs - row_dot) * scaling).astype(BF16)
                sum_o += dot(prob_low, v_h, 0, 0)
                sum_q += dot(grad, k_h, 0, 0)
                sum_v += dot(prob_low, ga_h, 1, 0)
                sum_k += dot(grad, q_h, 1, 0)
            at_ref[rows, cols] = sum_o.astype(BF16)
            gq_ref[rows, cols] = sum_q.astype(BF16)
        gk_ref[:, cols] = sum_k.astype(BF16)
        gv_ref[:, cols] = sum_v.astype(BF16)
        return carry

    lax.fori_loop(0, width // 128, pair, 0)
    for index, ref in enumerate((gq_ref, gk_ref, gv_ref)):
        raw_ref[index] = dot(ref[...], nor_ref[...], 0, 0).astype(BF16)
    raw_ref[3] = dot(u_ref[...], at_ref[...], 0, 0).astype(BF16)
    grad_normed = (
        dot(gq_ref[...], w_ref[0], 1, 0)
        + dot(gk_ref[...], w_ref[1], 1, 0)
        + dot(gv_ref[...], w_ref[2], 1, 0)
    )
    centred = cen_ref[...]
    gg_ref[...] = jnp.sum(grad_normed * centred, 0, keepdims=True)
    scaled = grad_normed * gain
    branch = inv_ref[...] * (
        scaled
        - jnp.mean(scaled, -1, keepdims=True)
        - centred * jnp.mean(scaled * centred, -1, keepdims=True)
    )
    gf_ref[...] = (u_ref[...].astype(F32) + branch.astype(BF16).astype(F32)).astype(BF16)


def row_back(f_row, u_row, w_full, gain):
    length, width = f_row.shape
    square = pltpu.VMEM((length, width), BF16)
    return pl.pallas_call(
        row_kernel,
        out_shape=(
            jax.ShapeDtypeStruct((length, width), BF16),
            jax.ShapeDtypeStruct((4, width, width), BF16),
            jax.ShapeDtypeStruct((1, width), F32),
        ),
        in_specs=[pl.BlockSpec(memory_space=pltpu.VMEM)] * 4,
        out_specs=[pl.BlockSpec(memory_space=pltpu.VMEM)] * 3,
        scratch_shapes=[
            pltpu.VMEM((length, width), F32),
            pltpu.VMEM((length, 1), F32),
        ]
        + [square] * 9,
        compiler_params=pltpu.CompilerParams(vmem_limit_bytes=48 << 20),
        name="row_back",
    )(f_row, u_row, w_full, gain)


def scatter_kernel(
    gf_ref, raw_ref, gg_ref, out_ref, gw_ref, gain_ref,
    got_c, acc_c, got_y, acc_y, got_x, acc_x, got_z,
    sum_c, sum_y, sum_x, sum_z, send, recv, local,
):
    grp, trk, z, x, y_hi, y_lo, core = position()
    enter(grp, trk, y_hi, y_lo, core, z, x)
    other = y_lo * NC + 1 - core
    y_at = y_hi * NYL + y_lo

    swaps = []
    for low in range(NYL):
        theirs = raw_ref.at[:, :, :, :, :, lanes(low * NC + 1 - core)]
        swaps.append(remote(theirs, got_c.at[low], send.at[1], recv.at[1], other, trk))
    sum_c[core] = gg_ref[...]
    swaps.append(remote(gg_ref, sum_c.at[core], send.at[5], recv.at[5], other, trk))
    for copy in swaps:
        copy.start()
    exchange_start(gf_ref, out_ref, send.at[0], recv.at[0], local, grp, trk)
    wait_all(got_c, send.at[1], recv.at[1], grp, trk)
    wait_all(sum_c.at[0], send.at[5], recv.at[5], grp, trk)
    for low in range(NYL):
        acc_c[low] = (
            raw_ref[:, :, :, :, :, lanes(low * NC + core)].astype(F32) + got_c[low].astype(F32)
        ).astype(BF16)
    sum_y[y_at] = sum_c[0] + sum_c[1]

    def y_peer(s):
        return (y_lo + s % 2) % NYL, (y_hi + s // 2) % NYH

    swaps = []
    for s in range(1, NYL * NYH):
        low, high = y_peer(s)
        to = (low * NC + core, trk_of(z, x, high))
        swaps.append(
            remote(acc_c.at[low, :, :, :, high], got_y.at[y_at], send.at[2], recv.at[2], *to)
        )
        swaps.append(remote(sum_y.at[y_at], sum_y.at[y_at], send.at[6], recv.at[6], *to))
    for copy in swaps:
        copy.start()
    wait_all(got_y.at[: NYL * NYH - 1], send.at[2], recv.at[2], grp, trk)
    wait_all(sum_y.at[: NYL * NYH - 1], send.at[6], recv.at[6], grp, trk)
    total = acc_c[y_lo, :, :, :, y_hi].astype(F32)
    for s in range(1, NYL * NYH):
        low, high = y_peer(s)
        total += got_y[high * NYL + low].astype(F32)
    acc_y[...] = total.astype(BF16)
    sum_x[x] = sum_y[0] + sum_y[1] + sum_y[2] + sum_y[3]

    swaps = []
    for s in range(1, NX):
        at = (x + s) % NX
        to = (grp, trk_of(z, at, y_hi))
        swaps.append(remote(acc_y.at[:, :, at], got_x.at[x], send.at[3], recv.at[3], *to))
        swaps.append(remote(sum_x.at[x], sum_x.at[x], send.at[7], recv.at[7], *to))
    for copy in swaps:
        copy.start()
    wait_all(got_x.at[: NX - 1], send.at[3], recv.at[3], grp, trk)
    wait_all(sum_x.at[: NX - 1], send.at[7], recv.at[7], grp, trk)
    total = acc_y[:, :, x].astype(F32)
    for s in range(1, NX):
        total += got_x[(x + s) % NX].astype(F32)
    acc_x[...] = total.astype(BF16)
    all_x = sum_x[0]
    for s in range(1, NX):
        all_x += sum_x[s]
    sum_z[z] = all_x

    swaps = []
    for s in range(1, NZ):
        at = (z + s) % NZ
        to = (grp, trk_of(at, x, y_hi))
        swaps.append(remote(acc_x.at[:, at], got_z.at[z], send.at[4], recv.at[4], *to))
        swaps.append(remote(sum_z.at[z], sum_z.at[z], send.at[8], recv.at[8], *to))
    for copy in swaps:
        copy.start()
    wait_all(got_z.at[: NZ - 1], send.at[4], recv.at[4], grp, trk)
    wait_all(sum_z.at[: NZ - 1], send.at[8], recv.at[8], grp, trk)
    total = acc_x[:, z].astype(F32)
    for s in range(1, NZ):
        total += got_z[(z + s) % NZ].astype(F32)
    gw_ref[...] = total
    all_z = sum_z[0]
    for s in range(1, NZ):
        all_z += sum_z[s]
    gain_ref[...] = all_z
    exchange_wait(gf_ref, out_ref, send.at[0], recv.at[0], local, grp, trk)


def scatter(gf_row, raw, gain_term):
    tracks, cells, width = gf_row.shape
    outs = raw.shape[4]
    any_, vmem = pl.BlockSpec(memory_space=pl.ANY), pl.BlockSpec(memory_space=pltpu.VMEM)
    return pl.pallas_call(
        scatter_kernel,
        out_shape=(
            jax.ShapeDtypeStruct((tracks, cells, width), BF16),
            jax.ShapeDtypeStruct((4, outs, 128), F32),
            jax.ShapeDtypeStruct((1, width), F32),
        ),
        in_specs=[any_, vmem, vmem],
        out_specs=[any_, vmem, vmem],
        scratch_shapes=[
            pltpu.VMEM((NYL, 4, NZ, NX, NYH, outs, 128), BF16),
            pltpu.VMEM((NYL, 4, NZ, NX, NYH, outs, 128), BF16),
            pltpu.VMEM((NYL * NYH, 4, NZ, NX, outs, 128), BF16),
            pltpu.VMEM((4, NZ, NX, outs, 128), BF16),
            pltpu.VMEM((NX, 4, NZ, outs, 128), BF16),
            pltpu.VMEM((4, NZ, outs, 128), BF16),
            pltpu.VMEM((NZ, 4, outs, 128), BF16),
            pltpu.VMEM((NC, 1, width), F32),
            pltpu.VMEM((NYL * NYH, 1, width), F32),
            pltpu.VMEM((NX, 1, width), F32),
            pltpu.VMEM((NZ, 1, width), F32),
            pltpu.SemaphoreType.DMA((9,)),
            pltpu.SemaphoreType.DMA((9,)),
            pltpu.SemaphoreType.DMA,
        ],
        compiler_params=pltpu.CompilerParams(
            collective_id=2, has_side_effects=True, vmem_limit_bytes=32 << 20
        ),
        name="scatter_grads",
    )(gf_row, raw, gain_term)


def shards(fields, upstream, ln_gain, weights):
    tracks, cells, width = fields.shape
    cell_count = tracks * lax.axis_size("grp") * cells * lax.axis_size("trk")
    w_tile = jnp.swapaxes(weights, 1, 2)
    f_row, u_row, w_full = gather(fields, upstream, w_tile)
    gf_row, raw, gain_term = row_back(
        f_row.reshape(tracks * cells, width),
        u_row.reshape(tracks * cells, width),
        w_full.reshape(4, width, width),
        ln_gain.reshape(1, width),
    )
    grad_fields, raw_part, gain_sum = scatter(
        gf_row.reshape(tracks, cells, width),
        raw.reshape(4, NZ, NX, NYH, w_tile.shape[1], width),
        gain_term,
    )
    factor = float(cell_count) ** (-0.5)
    return (
        grad_fields,
        jnp.swapaxes(raw_part, 1, 2) * factor,
        gain_sum.reshape(width) * factor,
    )


def solution(mesh):
    in_specs = (P("grp", "trk", None), P("grp", "trk", None), P(), P(None, "grp", "trk"))
    out_specs = (P("grp", "trk", None), P(None, "grp", "trk"), P())
    return jax.shard_map(shards, mesh=mesh, in_specs=in_specs, out_specs=out_specs, check_vma=False)
```

```python
import jax
import jax.numpy as jnp
from jax import lax
from jax.experimental import pallas as pl
from jax.experimental.pallas import tpu as pltpu
from jax.sharding import PartitionSpec as P

NZ, NX, NYH = 8, 4, 2
NYL, NC = 2, 2
HEAD = 64
MESH = pl.DeviceIdType.MESH
F32, BF16 = jnp.float32, jnp.bfloat16


def dot(a, b, ca, cb):
    return lax.dot_general(a, b, (((ca,), (cb,)), ((), ())), preferred_element_type=F32)


def position():
    grp, trk = lax.axis_index("grp"), lax.axis_index("trk")
    z, x, y_hi = trk // (NX * NYH), (trk // NYH) % NX, trk % NYH
    y_lo, core = grp // NC, grp % NC
    return grp, trk, z, x, y_hi, y_lo, core


def trk_of(z, x, y_hi):
    return (z * NX + x) * NYH + y_hi


def remote(src, dst, send, recv, grp, trk):
    return pltpu.make_async_remote_copy(
        src_ref=src, dst_ref=dst, send_sem=send, recv_sem=recv,
        device_id=(grp, trk), device_id_type=MESH,
    )


def landed(view, recv, grp, trk):
    remote(view, view, recv, recv, grp, trk).wait_recv()


def left(view, send, grp, trk):
    remote(view, view, send, send, grp, trk).wait_send()


def lanes(grp):
    return pl.ds(pl.multiple_of(grp * 128, 128), 128)


def flips(value, count, stride):
    bits = count.bit_length() - 1
    return [(1 - 2 * ((value // 2**b) % 2)) * (2**b * stride) for b in range(bits)]


def row_kernel(
    f_ref, u_ref, w_ref, gain_ref, out_ref, gw_ref, gg_ref,
    fr, ur, wf, wt, cen_ref, inv_ref, prob_ref,
    up, nor, qr, kr, vr, gar, atr, gqr, gkr, gvr, branch,
    raw, got_c, acc_c, got_y, acc_y, got_x, acc_x, got_z,
    sum_c, sum_y, sum_x, sum_z,
    near, local, send_a, recv_a, send_w, recv_w, send_g, recv_g, send_s, recv_s,
):
    grp, trk, z, x, y_hi, y_lo, core = position()
    tracks, cells, width = f_ref.shape
    length = tracks * cells
    plane = NX * NYH
    ny = NYL * NYH
    y_at = y_hi * NYL + y_lo
    sibling = y_lo * NC + 1 - core

    def y_peer(s):
        return (y_lo + s % 2) % NYL, (y_hi + s // 2) % NYH

    z_peers = [(grp, trk_of((z + s) % NZ, x, y_hi)) for s in range(1, NZ)]
    x_peers = [(grp, trk_of(z, (x + s) % NX, y_hi)) for s in range(1, NX)]
    y_peers = []
    for s in range(1, ny):
        low, high = y_peer(s)
        y_peers.append((low * NC + core, trk_of(z, x, high)))

    barrier = pltpu.get_barrier_semaphore()
    greeted = z_peers + x_peers + y_peers + [(sibling, trk)]
    for peer in greeted:
        pl.semaphore_signal(barrier, inc=1, device_id=peer, device_id_type=MESH)
    pl.semaphore_wait(barrier, len(greeted))

    mine = wf.at[:, z, x, y_hi, :, lanes(grp)]
    own = pltpu.make_async_copy(w_ref, mine, local.at[2])
    own.start()
    for peer in z_peers:
        remote(w_ref, mine, send_w.at[0], recv_w.at[0], *peer).start()

    for peer in x_peers:
        pl.semaphore_signal(near.at[0], inc=1, device_id=peer, device_id_type=MESH)
    pl.semaphore_wait(near.at[0], len(x_peers))
    pl.semaphore_signal(
        near.at[1], inc=1, device_id=(grp, trk_of(z, x, 1 - y_hi)), device_id_type=MESH
    )
    pl.semaphore_wait(near.at[1], 1)

    in_plane = flips(trk % plane, plane, 1)
    over_z = flips(z, NZ, plane)
    offsets = []
    for k in range(plane):
        offset = trk * 0
        for b, flip in enumerate(in_plane):
            if (k >> b) & 1:
                offset = offset + flip
        offsets.append(offset)

    def exchange(src, dst, at, first, last):
        def some(high, skip):
            base = trk
            for b, flip in enumerate(over_z):
                base = base + ((high // 2**b) % 2) * flip
            for k in range(skip, plane):
                to = base + offsets[k]
                remote(src.at[to], dst.at[trk], send_a.at[at], recv_a.at[at], grp, to).start()

        def step(high, carry):
            some(high, 0)
            return carry

        if first == 0:
            pltpu.make_async_copy(src.at[trk], dst.at[trk], local.at[min(at, 1)]).start()
            some(0, 1)
            first = 1
        lax.fori_loop(first, last, step, 0)

    def exchanged(src, dst, at):
        landed(dst.at[: tracks - 1], recv_a.at[at], grp, trk)
        pltpu.make_async_copy(src.at[trk], dst.at[trk], local.at[min(at, 1)]).wait()

    exchange(f_ref, fr, 0, 0, NZ // 4)
    own.wait()
    landed(wf.at[:, : NZ - 1, 0, 0, :, :128], recv_w.at[0], grp, trk)
    column = wf.at[:, :, x, y_hi, :, lanes(grp)]
    for peer in x_peers:
        remote(column, column, send_w.at[1], recv_w.at[1], *peer).start()
    exchange(f_ref, fr, 0, NZ // 4, NZ // 2)
    landed(wf.at[:, :, : NX - 1, 0, :, :128], recv_w.at[1], grp, trk)
    for m in range(4):
        part = wf.at[m, :, :, y_hi, :, lanes(grp)]
        for peer in y_peers:
            remote(part, part, send_w.at[2 + m], recv_w.at[2 + m], *peer).start()
    exchange(f_ref, fr, 0, NZ // 2, NZ)

    def swap_weights(m):
        landed(wf.at[m, :, :, 0, :, : (ny - 1) * 128], recv_w.at[2 + m], grp, trk)
        for low in range(NYL):
            half = wf.at[m, :, :, :, :, lanes(low * NC + core)]
            remote(half, half, send_w.at[6 + m], recv_w.at[6 + m], sibling, trk).start()

    def take_weights(m):
        landed(wf.at[m, :, :, :, :, : NYL * 128], recv_w.at[6 + m], grp, trk)
        wt[m] = wf[m].astype(F32).reshape(width, width).astype(BF16)

    for m in range(3):
        swap_weights(m)
    exchange(u_ref, ur, 1, 0, NZ)
    swap_weights(3)

    gain = gain_ref[...]
    exchanged(f_ref, fr, 0)
    values = fr[...].astype(F32).reshape(length, width)
    offset = values - jnp.mean(values, -1, keepdims=True)
    inv_std = lax.rsqrt(jnp.mean(offset * offset, -1, keepdims=True) + 1e-05)
    centred = offset * inv_std
    cen_ref[...] = centred
    inv_ref[...] = inv_std
    nor[...] = (centred * gain).astype(BF16)
    scaling = HEAD ** (-0.5)
    for m, ref in enumerate((qr, kr, vr)):
        take_weights(m)
        ref[...] = dot(nor[...], wt[m], 1, 1).astype(BF16)
    half = length // 2
    lane = lax.broadcasted_iota(jnp.int32, (1, 128), 1)
    masks = [((lane >= h * HEAD) & (lane < (h + 1) * HEAD)).astype(BF16) for h in range(2)]
    pairs = width // 128

    def forward(pair, carry):
        cols = lanes(pair)
        q, k, v = qr[:, cols], kr[:, cols], vr[:, cols]
        for part in range(2):
            rows = slice(part * half, (part + 1) * half)
            sum_o = jnp.zeros((half, 128), F32)
            for h in range(2):
                scores = dot(k * masks[h], q[rows], 1, 1) * scaling
                shifted = jnp.exp(scores - jnp.max(scores, 0, keepdims=True))
                prob = shifted * (1.0 / jnp.sum(shifted, 0, keepdims=True))
                prob_ref[2 * pair + h, part] = prob
                sum_o += dot(prob.astype(BF16), v * masks[h], 0, 0)
            atr[rows, cols] = sum_o.astype(BF16)
        return carry

    lax.fori_loop(0, pairs, forward, 0)

    def chunk(c):
        if c == 0:
            return slice(3, 4), slice(0, NZ)
        return slice(0, 3), slice((c - 1) * NZ // pairs, c * NZ // pairs)

    def core_start(c):
        ms, zs = chunk(c)
        for low in range(NYL):
            theirs = raw.at[ms, zs, :, :, :, lanes(low * NC + 1 - core)]
            remote(
                theirs, got_c.at[low, ms, zs], send_g.at[0, c], recv_g.at[0, c], sibling, trk
            ).start()

    def core_finish(c):
        ms, zs = chunk(c)
        landed(got_c.at[:, ms, zs], recv_g.at[0, c], grp, trk)
        for low in range(NYL):
            acc_c[low, ms, zs] = (
                raw[ms, zs, :, :, :, lanes(low * NC + core)].astype(F32)
                + got_c[low, ms, zs].astype(F32)
            ).astype(BF16)
        for s in range(1, ny):
            low, high = y_peer(s)
            remote(
                acc_c.at[low, ms, zs, :, high], got_y.at[y_at, ms, zs],
                send_g.at[1, c], recv_g.at[1, c], *y_peers[s - 1],
            ).start()

    def y_finish(c):
        ms, zs = chunk(c)
        landed(got_y.at[: ny - 1, ms, zs], recv_g.at[1, c], grp, trk)
        total = acc_c[y_lo, ms, zs, :, y_hi].astype(F32)
        for s in range(1, ny):
            low, high = y_peer(s)
            total += got_y[high * NYL + low, ms, zs].astype(F32)
        acc_y[ms, zs] = total.astype(BF16)
        for s in range(1, NX):
            remote(
                acc_y.at[ms, zs, (x + s) % NX], got_x.at[x, ms, zs],
                send_g.at[2, c], recv_g.at[2, c], *x_peers[s - 1],
            ).start()

    def x_finish(c):
        ms, zs = chunk(c)
        landed(got_x.at[: NX - 1, ms, zs], recv_g.at[2, c], grp, trk)
        total = acc_y[ms, zs, x].astype(F32)
        for s in range(1, NX):
            total += got_x[(x + s) % NX, ms, zs].astype(F32)
        acc_x[ms, zs] = total.astype(BF16)

    raw_tiles = raw.shape[2:]

    exchanged(u_ref, ur, 1)
    up[...] = ur[...].astype(F32).reshape(length, width).astype(BF16)
    take_weights(3)
    gar[...] = dot(up[...], wt[3], 1, 0).astype(BF16)
    raw[3] = dot(up[...], atr[...], 0, 0).reshape(raw.shape[1:]).astype(BF16)
    core_start(0)
    for pair in range(pairs):
        cols = slice(pair * 128, (pair + 1) * 128)
        q, k, v, ga = qr[:, cols], kr[:, cols], vr[:, cols], gar[:, cols]
        sum_k = jnp.zeros((length, 128), F32)
        sum_v = jnp.zeros((length, 128), F32)
        for part in range(2):
            rows = slice(part * half, (part + 1) * half)
            sum_q = jnp.zeros((half, 128), F32)
            for h in range(2):
                prob = prob_ref[2 * pair + h, part]
                dprobs = dot(v * masks[h], ga[rows], 1, 1)
                row_dot = jnp.sum(prob * dprobs, 0, keepdims=True)
                grad = (prob * (dprobs - row_dot) * scaling).astype(BF16)
                sum_q += dot(grad, k * masks[h], 0, 0)
                sum_v += dot(prob.astype(BF16), ga[rows] * masks[h], 1, 0)
                sum_k += dot(grad, q[rows] * masks[h], 1, 0)
            gqr[rows, cols] = sum_q.astype(BF16)
        gkr[:, cols] = sum_k.astype(BF16)
        gvr[:, cols] = sum_v.astype(BF16)
        zs = chunk(pair + 1)[1]
        for m, ref in enumerate((gqr, gkr, gvr)):
            piece = dot(ref[:, cols], nor[...], 0, 0)
            raw[m, zs] = piece.reshape((zs.stop - zs.start,) + raw_tiles).astype(BF16)
        core_start(pair + 1)
        core_finish(pair)
        if pair >= 1:
            y_finish(pair - 1)
        if pair >= 2:
            x_finish(pair - 2)
    grad_normed = (
        dot(gqr[...], wt[0], 1, 0) + dot(gkr[...], wt[1], 1, 0) + dot(gvr[...], wt[2], 1, 0)
    )
    centred = cen_ref[...]
    sum_c[core] = jnp.sum(grad_normed * centred, 0, keepdims=True)
    remote(sum_c.at[core], sum_c.at[core], send_s.at[0], recv_s.at[0], sibling, trk).start()
    core_finish(pairs)
    scaled = grad_normed * gain
    grad = inv_ref[...] * (
        scaled
        - jnp.mean(scaled, -1, keepdims=True)
        - centred * jnp.mean(scaled * centred, -1, keepdims=True)
    )
    branch[...] = grad.reshape(tracks, cells, width).astype(BF16)
    landed(sum_c.at[0], recv_s.at[0], grp, trk)
    sum_y[y_at] = sum_c[0] + sum_c[1]
    for peer in y_peers:
        remote(sum_y.at[y_at], sum_y.at[y_at], send_s.at[1], recv_s.at[1], *peer).start()
    exchange(branch, out_ref, 2, 0, NZ // 2)
    y_finish(pairs - 1)
    x_finish(pairs - 2)
    landed(sum_y.at[: ny - 1], recv_s.at[1], grp, trk)
    all_y = sum_y[0]
    for s in range(1, ny):
        all_y += sum_y[s]
    sum_x[x] = all_y
    for peer in x_peers:
        remote(sum_x.at[x], sum_x.at[x], send_s.at[2], recv_s.at[2], *peer).start()
    y_finish(pairs)
    exchange(branch, out_ref, 2, NZ // 2, NZ)
    x_finish(pairs - 1)
    x_finish(pairs)
    for s in range(1, NZ):
        remote(
            acc_x.at[:, (z + s) % NZ], got_z.at[z], send_g.at[3, 0], recv_g.at[3, 0],
            *z_peers[s - 1],
        ).start()
    landed(sum_x.at[: NX - 1], recv_s.at[2], grp, trk)
    all_x = sum_x[0]
    for s in range(1, NX):
        all_x += sum_x[s]
    sum_z[z] = all_x
    for peer in z_peers:
        remote(sum_z.at[z], sum_z.at[z], send_s.at[3], recv_s.at[3], *peer).start()
    landed(got_z.at[: NZ - 1], recv_g.at[3, 0], grp, trk)
    total = acc_x[:, z].astype(F32)
    for s in range(1, NZ):
        total += got_z[(z + s) % NZ].astype(F32)
    gw_ref[...] = total
    landed(sum_z.at[: NZ - 1], recv_s.at[3], grp, trk)
    all_z = sum_z[0]
    for s in range(1, NZ):
        all_z += sum_z[s]
    gg_ref[...] = all_z
    exchanged(branch, out_ref, 2)

    for at in range(3):
        left(out_ref.at[: tracks - 1], send_a.at[at], grp, trk)
    left(wf.at[:, : NZ - 1, 0, 0, :, :128], send_w.at[0], grp, trk)
    left(wf.at[:, :, : NX - 1, 0, :, :128], send_w.at[1], grp, trk)
    for m in range(4):
        left(wf.at[m, :, :, 0, :, : (ny - 1) * 128], send_w.at[2 + m], grp, trk)
        left(wf.at[m, :, :, :, :, : NYL * 128], send_w.at[6 + m], grp, trk)
    for c in range(pairs + 1):
        ms, zs = chunk(c)
        left(got_c.at[:, ms, zs], send_g.at[0, c], grp, trk)
        left(got_y.at[: ny - 1, ms, zs], send_g.at[1, c], grp, trk)
        left(got_x.at[: NX - 1, ms, zs], send_g.at[2, c], grp, trk)
    left(got_z.at[: NZ - 1], send_g.at[3, 0], grp, trk)
    left(sum_c.at[0], send_s.at[0], grp, trk)
    left(sum_y.at[: ny - 1], send_s.at[1], grp, trk)
    left(sum_x.at[: NX - 1], send_s.at[2], grp, trk)
    left(sum_z.at[: NZ - 1], send_s.at[3], grp, trk)


def layer_back(fields, upstream, w_tile, gain):
    tracks, cells, width = fields.shape
    outs = w_tile.shape[1]
    length = tracks * cells
    ny = NYL * NYH
    any_, vmem = pl.BlockSpec(memory_space=pl.ANY), pl.BlockSpec(memory_space=pltpu.VMEM)
    dma = pltpu.SemaphoreType.DMA
    square = pltpu.VMEM((length, width), BF16)
    row = pltpu.VMEM((tracks, cells, width), BF16)
    return pl.pallas_call(
        row_kernel,
        out_shape=(
            jax.ShapeDtypeStruct((tracks, cells, width), BF16),
            jax.ShapeDtypeStruct((4, outs, 128), F32),
            jax.ShapeDtypeStruct((1, width), F32),
        ),
        in_specs=[any_, any_, any_, vmem],
        out_specs=[any_, vmem, vmem],
        scratch_shapes=[
            row,
            row,
            pltpu.VMEM((4, NZ, NX, NYH, outs, width), BF16),
            pltpu.VMEM((4, width, width), BF16),
            pltpu.VMEM((length, width), F32),
            pltpu.VMEM((length, 1), F32),
            pltpu.VMEM((width // HEAD, 2, length, length // 2), F32),
        ]
        + [square] * 10
        + [
            row,
            pltpu.VMEM((4, NZ, NX, NYH, outs, width), BF16),
            pltpu.VMEM((NYL, 4, NZ, NX, NYH, outs, 128), BF16),
            pltpu.VMEM((NYL, 4, NZ, NX, NYH, outs, 128), BF16),
            pltpu.VMEM((ny, 4, NZ, NX, outs, 128), BF16),
            pltpu.VMEM((4, NZ, NX, outs, 128), BF16),
            pltpu.VMEM((NX, 4, NZ, outs, 128), BF16),
            pltpu.VMEM((4, NZ, outs, 128), BF16),
            pltpu.VMEM((NZ, 4, outs, 128), BF16),
            pltpu.VMEM((NC, 1, width), F32),
            pltpu.VMEM((ny, 1, width), F32),
            pltpu.VMEM((NX, 1, width), F32),
            pltpu.VMEM((NZ, 1, width), F32),
            pltpu.SemaphoreType.REGULAR((2,)),
            dma((3,)),
            dma((3,)),
            dma((3,)),
            dma((10,)),
            dma((10,)),
            dma((4, 5)),
            dma((4, 5)),
            dma((4,)),
            dma((4,)),
        ],
        compiler_params=pltpu.CompilerParams(
            collective_id=1, has_side_effects=True, vmem_limit_bytes=56 << 20
        ),
        name="layer_back",
    )(fields, upstream, w_tile, gain)


def shards(fields, upstream, ln_gain, weights):
    tracks, cells, width = fields.shape
    cell_count = tracks * lax.axis_size("grp") * cells * lax.axis_size("trk")
    w_tile = jnp.swapaxes(weights, 1, 2)
    branch, raw_part, gain_sum = layer_back(fields, upstream, w_tile, ln_gain.reshape(1, width))
    factor = float(cell_count) ** (-0.5)
    return (
        (upstream.astype(F32) + branch.astype(F32)).astype(BF16),
        jnp.swapaxes(raw_part, 1, 2) * factor,
        gain_sum.reshape(width) * factor,
    )


def solution(mesh):
    in_specs = (P("grp", "trk", None), P("grp", "trk", None), P(), P(None, "grp", "trk"))
    out_specs = (P("grp", "trk", None), P(None, "grp", "trk"), P())
    return jax.shard_map(shards, mesh=mesh, in_specs=in_specs, out_specs=out_specs, check_vma=False)
```

```python
import jax
import jax.numpy as jnp
from jax import lax
from jax.experimental import pallas as pl
from jax.experimental.pallas import tpu as pltpu
from jax.sharding import PartitionSpec as P

NZ, NX, NYH = 8, 4, 2
NYL, NC = 2, 2
HEAD = 64
MESH = pl.DeviceIdType.MESH
F32, BF16 = jnp.float32, jnp.bfloat16


def dot(a, b, ca, cb):
    return lax.dot_general(a, b, (((ca,), (cb,)), ((), ())), preferred_element_type=F32)


def position():
    grp, trk = lax.axis_index("grp"), lax.axis_index("trk")
    z, x, y_hi = trk // (NX * NYH), (trk // NYH) % NX, trk % NYH
    y_lo, core = grp // NC, grp % NC
    return grp, trk, z, x, y_hi, y_lo, core


def trk_of(z, x, y_hi):
    return (z * NX + x) * NYH + y_hi


def remote(src, dst, send, recv, grp, trk):
    return pltpu.make_async_remote_copy(
        src_ref=src, dst_ref=dst, send_sem=send, recv_sem=recv,
        device_id=(grp, trk), device_id_type=MESH,
    )


def landed(view, recv, grp, trk):
    remote(view, view, recv, recv, grp, trk).wait_recv()


def left(view, send, grp, trk):
    remote(view, view, send, send, grp, trk).wait_send()


def lanes(grp):
    return pl.ds(pl.multiple_of(grp * 128, 128), 128)


def flips(value, count, stride):
    bits = count.bit_length() - 1
    return [(1 - 2 * ((value // 2**b) % 2)) * (2**b * stride) for b in range(bits)]


def row_kernel(
    f_ref, u_ref, w_ref, gain_ref, out_ref, gw_ref, gg_ref,
    fs, us, fr, ur, wf, wt, cen_ref, inv_ref, prob_ref,
    up, nor, qr, kr, vr, gar, atr, gqr, gkr, gvr, branch,
    raw, got_c, acc_c, got_y, acc_y, got_x, got_xf, acc_xf, got_yl, acc, got_z,
    sum_c, sum_y, sum_x, sum_z,
    local, send_a, recv_a, send_w, recv_w, send_g, recv_g, send_s, recv_s,
):
    grp, trk, z, x, y_hi, y_lo, core = position()
    tracks, cells, width = f_ref.shape
    length = tracks * cells
    plane = NX * NYH
    ny = NYL * NYH
    y_at = y_hi * NYL + y_lo
    sibling = y_lo * NC + 1 - core

    def y_peer(s):
        return (y_lo + s % 2) % NYL, (y_hi + s // 2) % NYH

    z_peers = [(grp, trk_of((z + s) % NZ, x, y_hi)) for s in range(1, NZ)]
    x_peers = [(grp, trk_of(z, (x + s) % NX, y_hi)) for s in range(1, NX)]
    y_peers = []
    for s in range(1, ny):
        low, high = y_peer(s)
        y_peers.append((low * NC + core, trk_of(z, x, high)))

    loads = [
        pltpu.make_async_copy(src, dst, local.at[3 + i])
        for i, (src, dst) in enumerate(((f_ref, fs), (u_ref, us)))
    ]
    for load in loads:
        load.start()
    mine = wf.at[:, z, x, y_hi, :, lanes(grp)]
    own = pltpu.make_async_copy(w_ref, mine, local.at[2])
    own.start()

    barrier = pltpu.get_barrier_semaphore()

    def greet(step, carry):
        to = lax.rem(trk + tracks // 2 + step, tracks)
        pl.semaphore_signal(barrier, inc=1, device_id=(grp, to), device_id_type=MESH)
        return carry

    lax.fori_loop(0, tracks // 2, greet, 0)
    lax.fori_loop(tracks // 2 + 1, tracks, greet, 0)
    for peer in y_peers:
        pl.semaphore_signal(barrier, inc=1, device_id=peer, device_id_type=MESH)
    pl.semaphore_signal(barrier, inc=1, device_id=(sibling, trk), device_id_type=MESH)
    pl.semaphore_wait(barrier, tracks - 1 + len(y_peers) + 1)

    for peer in z_peers:
        remote(w_ref, mine, send_w.at[0], recv_w.at[0], *peer).start()
    for load in loads:
        load.wait()

    in_plane = flips(trk % plane, plane, 1)
    over_z = flips(z, NZ, plane)
    offsets = []
    for k in range(plane):
        offset = trk * 0
        for b, flip in enumerate(in_plane):
            if (k >> b) & 1:
                offset = offset + flip
        offsets.append(offset)

    def exchange(src, dst, at, first, last):
        def some(high, skip):
            base = trk
            for b, flip in enumerate(over_z):
                base = base + ((high // 2**b) % 2) * flip
            for k in range(skip, plane):
                to = base + offsets[k]
                remote(src.at[to], dst.at[trk], send_a.at[at], recv_a.at[at], grp, to).start()

        def step(high, carry):
            some(high, 0)
            return carry

        if first == 0:
            pltpu.make_async_copy(src.at[trk], dst.at[trk], local.at[min(at, 1)]).start()
            some(0, 1)
            first = 1
        lax.fori_loop(first, last, step, 0)

    def exchanged(src, dst, at):
        landed(dst.at[: tracks - 1], recv_a.at[at], grp, trk)
        pltpu.make_async_copy(src.at[trk], dst.at[trk], local.at[min(at, 1)]).wait()

    exchange(fs, fr, 0, 0, NZ)
    own.wait()
    landed(wf.at[:, : NZ - 1, 0, 0, :, :128], recv_w.at[0], grp, trk)
    by_x = wf.at[:2, :, x, y_hi, :, lanes(grp)]
    by_y = wf.at[2:, :, x, y_hi, :, lanes(grp)]
    for peer in x_peers:
        remote(by_x, by_x, send_w.at[1], recv_w.at[1], *peer).start()
    for peer in y_peers:
        remote(by_y, by_y, send_w.at[10], recv_w.at[10], *peer).start()
    exchange(us, ur, 1, 0, NZ // 2)
    landed(wf.at[:2, :, : NX - 1, 0, :, :128], recv_w.at[1], grp, trk)
    landed(wf.at[2:, :, 0, 0, :, : (ny - 1) * 128], recv_w.at[10], grp, trk)
    for m in (0, 2, 1, 3):
        if m < 2:
            part = wf.at[m, :, :, y_hi, :, lanes(grp)]
            for peer in y_peers:
                remote(part, part, send_w.at[2 + m], recv_w.at[2 + m], *peer).start()
        else:
            for s in range(ny):
                low, high = y_peer(s)
                part = wf.at[m, :, x, high, :, lanes(low * NC + core)]
                for peer in x_peers:
                    remote(part, part, send_w.at[2 + m], recv_w.at[2 + m], *peer).start()
    exchange(us, ur, 1, NZ // 2, NZ)

    def last_stage(m):
        if m < 2:
            return wf.at[m, :, :, 0, :, : (ny - 1) * 128]
        return wf.at[m, :, : NX - 1, :, :, : ny // NYH * 128]

    def swap_weights(m):
        landed(last_stage(m), recv_w.at[2 + m], grp, trk)
        for low in range(NYL):
            half = wf.at[m, :, :, :, :, lanes(low * NC + core)]
            remote(half, half, send_w.at[6 + m], recv_w.at[6 + m], sibling, trk).start()

    def take_weights(m):
        landed(wf.at[m, :, :, :, :, : NYL * 128], recv_w.at[6 + m], grp, trk)
        wt[m] = wf[m].astype(F32).reshape(width, width).astype(BF16)

    for m in (0, 2, 1, 3):
        swap_weights(m)

    gain = gain_ref[...]
    exchanged(fs, fr, 0)
    values = fr[...].astype(F32).reshape(length, width)
    offset = values - jnp.mean(values, -1, keepdims=True)
    inv_std = lax.rsqrt(jnp.mean(offset * offset, -1, keepdims=True) + 1e-05)
    centred = offset * inv_std
    cen_ref[...] = centred
    inv_ref[...] = inv_std
    nor[...] = (centred * gain).astype(BF16)
    scaling = HEAD ** (-0.5)
    for m, ref in ((0, qr), (2, vr), (1, kr)):
        take_weights(m)
        ref[...] = dot(nor[...], wt[m], 1, 1).astype(BF16)
    half = length // 2
    lane = lax.broadcasted_iota(jnp.int32, (1, 128), 1)
    masks = [((lane >= h * HEAD) & (lane < (h + 1) * HEAD)).astype(BF16) for h in range(2)]
    pairs = width // 128

    def forward(pair, carry):
        cols = lanes(pair)
        q, k, v = qr[:, cols], kr[:, cols], vr[:, cols]
        for part in range(2):
            rows = slice(part * half, (part + 1) * half)
            sum_o = jnp.zeros((half, 128), F32)
            for h in range(2):
                scores = dot(k * masks[h], q[rows], 1, 1) * scaling
                shifted = jnp.exp(scores - jnp.max(scores, 0, keepdims=True))
                prob = shifted * (1.0 / jnp.sum(shifted, 0, keepdims=True))
                prob_ref[2 * pair + h, part] = prob
                sum_o += dot(prob.astype(BF16), v * masks[h], 0, 0)
            atr[rows, cols] = sum_o.astype(BF16)
        return carry

    lax.fori_loop(0, pairs, forward, 0)

    def chunk(c):
        if c == 0:
            return slice(3, 4), slice(0, NZ)
        return slice(0, 3), slice((c - 1) * NZ // pairs, c * NZ // pairs)

    def y_first(c):
        return c > 0, slice(0, 2), chunk(c)[1]

    def x_first(c):
        return slice(2, 3) if c > 0 else slice(3, 4), chunk(c)[1]

    def core_start(c):
        ms, zs = chunk(c)
        for low in range(NYL):
            theirs = raw.at[ms, zs, :, :, :, lanes(low * NC + 1 - core)]
            remote(
                theirs, got_c.at[low, ms, zs], send_g.at[0, c], recv_g.at[0, c], sibling, trk
            ).start()

    def core_finish(c):
        ms, zs = chunk(c)
        landed(got_c.at[:, ms, zs], recv_g.at[0, c], grp, trk)
        for low in range(NYL):
            acc_c[low, ms, zs] = (
                raw[ms, zs, :, :, :, lanes(low * NC + core)].astype(F32)
                + got_c[low, ms, zs].astype(F32)
            ).astype(BF16)
        there, ms, zs = y_first(c)
        if there:
            for s in range(1, ny):
                low, high = y_peer(s)
                remote(
                    acc_c.at[low, ms, zs, :, high], got_y.at[y_at, ms, zs],
                    send_g.at[1, c], recv_g.at[1, c], *y_peers[s - 1],
                ).start()
        ms, zs = x_first(c)
        for s in range(1, NX):
            remote(
                acc_c.at[:, ms, zs, (x + s) % NX], got_xf.at[x, :, ms, zs],
                send_g.at[2, c], recv_g.at[2, c], *x_peers[s - 1],
            ).start()

    def second_start(c):
        there, ms, zs = y_first(c)
        if there:
            landed(got_y.at[: ny - 1, ms, zs], recv_g.at[1, c], grp, trk)
            total = acc_c[y_lo, ms, zs, :, y_hi].astype(F32)
            for s in range(1, ny):
                low, high = y_peer(s)
                total += got_y[high * NYL + low, ms, zs].astype(F32)
            acc_y[ms, zs] = total.astype(BF16)
            for s in range(1, NX):
                remote(
                    acc_y.at[ms, zs, (x + s) % NX], got_x.at[x, ms, zs],
                    send_g.at[3, c], recv_g.at[3, c], *x_peers[s - 1],
                ).start()
        ms, zs = x_first(c)
        landed(got_xf.at[: NX - 1, :, ms, zs], recv_g.at[2, c], grp, trk)
        total = acc_c[:, ms, zs, x].astype(F32)
        for s in range(1, NX):
            total += got_xf[(x + s) % NX, :, ms, zs].astype(F32)
        acc_xf[:, ms, zs] = total.astype(BF16)
        for s in range(1, ny):
            low, high = y_peer(s)
            remote(
                acc_xf.at[low, ms, zs, high], got_yl.at[y_at, ms, zs],
                send_g.at[4, c], recv_g.at[4, c], *y_peers[s - 1],
            ).start()

    def second_finish(c):
        there, ms, zs = y_first(c)
        if there:
            landed(got_x.at[: NX - 1, ms, zs], recv_g.at[3, c], grp, trk)
            total = acc_y[ms, zs, x].astype(F32)
            for s in range(1, NX):
                total += got_x[(x + s) % NX, ms, zs].astype(F32)
            acc[ms, zs] = total.astype(BF16)
        ms, zs = x_first(c)
        landed(got_yl.at[: ny - 1, ms, zs], recv_g.at[4, c], grp, trk)
        total = acc_xf[y_lo, ms, zs, y_hi].astype(F32)
        for s in range(1, ny):
            low, high = y_peer(s)
            total += got_yl[high * NYL + low, ms, zs].astype(F32)
        acc[ms, zs] = total.astype(BF16)

    raw_tiles = raw.shape[2:]

    exchanged(us, ur, 1)
    up[...] = ur[...].astype(F32).reshape(length, width).astype(BF16)
    take_weights(3)
    gar[...] = dot(up[...], wt[3], 1, 0).astype(BF16)
    raw[3] = dot(up[...], atr[...], 0, 0).reshape(raw.shape[1:]).astype(BF16)
    core_start(0)
    for pair in range(pairs):
        cols = slice(pair * 128, (pair + 1) * 128)
        q, k, v, ga = qr[:, cols], kr[:, cols], vr[:, cols], gar[:, cols]
        sum_k = jnp.zeros((length, 128), F32)
        sum_v = jnp.zeros((length, 128), F32)
        for part in range(2):
            rows = slice(part * half, (part + 1) * half)
            sum_q = jnp.zeros((half, 128), F32)
            for h in range(2):
                prob = prob_ref[2 * pair + h, part]
                dprobs = dot(v * masks[h], ga[rows], 1, 1)
                row_dot = jnp.sum(prob * dprobs, 0, keepdims=True)
                grad = (prob * (dprobs - row_dot) * scaling).astype(BF16)
                sum_q += dot(grad, k * masks[h], 0, 0)
                sum_v += dot(prob.astype(BF16), ga[rows] * masks[h], 1, 0)
                sum_k += dot(grad, q[rows] * masks[h], 1, 0)
            gqr[rows, cols] = sum_q.astype(BF16)
        gkr[:, cols] = sum_k.astype(BF16)
        gvr[:, cols] = sum_v.astype(BF16)
        zs = chunk(pair + 1)[1]
        for m, ref in enumerate((gqr, gkr, gvr)):
            piece = dot(ref[:, cols], nor[...], 0, 0)
            raw[m, zs] = piece.reshape((zs.stop - zs.start,) + raw_tiles).astype(BF16)
        core_start(pair + 1)
        core_finish(pair)
        if pair >= 2:
            second_start(pair - 2)
    grad_normed = (
        dot(gqr[...], wt[0], 1, 0) + dot(gkr[...], wt[1], 1, 0) + dot(gvr[...], wt[2], 1, 0)
    )
    centred = cen_ref[...]
    sum_c[core] = jnp.sum(grad_normed * centred, 0, keepdims=True)
    remote(sum_c.at[core], sum_c.at[core], send_s.at[0], recv_s.at[0], sibling, trk).start()
    core_finish(pairs)
    scaled = grad_normed * gain
    grad = inv_ref[...] * (
        scaled
        - jnp.mean(scaled, -1, keepdims=True)
        - centred * jnp.mean(scaled * centred, -1, keepdims=True)
    )
    grad = up[...].astype(F32) + grad.astype(BF16).astype(F32)
    branch[...] = grad.reshape(tracks, cells, width).astype(BF16)
    landed(sum_c.at[0], recv_s.at[0], grp, trk)
    sum_y[y_at] = sum_c[0] + sum_c[1]
    for peer in y_peers:
        remote(sum_y.at[y_at], sum_y.at[y_at], send_s.at[1], recv_s.at[1], *peer).start()
    exchange(branch, out_ref, 2, 0, NZ // 2)
    for c in range(pairs - 2, pairs):
        second_start(c)
    exchange(branch, out_ref, 2, NZ // 2, NZ)
    landed(sum_y.at[: ny - 1], recv_s.at[1], grp, trk)
    all_y = sum_y[0]
    for s in range(1, ny):
        all_y += sum_y[s]
    sum_x[x] = all_y
    for peer in x_peers:
        remote(sum_x.at[x], sum_x.at[x], send_s.at[2], recv_s.at[2], *peer).start()
    second_start(pairs)
    for c in range(pairs + 1):
        second_finish(c)
    for s in range(1, NZ):
        remote(
            acc.at[:, (z + s) % NZ], got_z.at[z], send_g.at[5, 0], recv_g.at[5, 0],
            *z_peers[s - 1],
        ).start()
    landed(sum_x.at[: NX - 1], recv_s.at[2], grp, trk)
    all_x = sum_x[0]
    for s in range(1, NX):
        all_x += sum_x[s]
    sum_z[z] = all_x
    for peer in z_peers:
        remote(sum_z.at[z], sum_z.at[z], send_s.at[3], recv_s.at[3], *peer).start()
    landed(got_z.at[: NZ - 1], recv_g.at[5, 0], grp, trk)
    total = acc[:, z].astype(F32)
    for s in range(1, NZ):
        total += got_z[(z + s) % NZ].astype(F32)
    factor = float(length * lax.axis_size("grp") * tracks) ** (-0.5)
    gw_ref[...] = total * factor
    landed(sum_z.at[: NZ - 1], recv_s.at[3], grp, trk)
    all_z = sum_z[0]
    for s in range(1, NZ):
        all_z += sum_z[s]
    gg_ref[...] = all_z * factor
    exchanged(branch, out_ref, 2)

    for at in range(3):
        left(out_ref.at[: tracks - 1], send_a.at[at], grp, trk)
    left(wf.at[:, : NZ - 1, 0, 0, :, :128], send_w.at[0], grp, trk)
    left(wf.at[:2, :, : NX - 1, 0, :, :128], send_w.at[1], grp, trk)
    left(wf.at[2:, :, 0, 0, :, : (ny - 1) * 128], send_w.at[10], grp, trk)
    for m in range(4):
        left(last_stage(m), send_w.at[2 + m], grp, trk)
        left(wf.at[m, :, :, :, :, : NYL * 128], send_w.at[6 + m], grp, trk)
    for c in range(pairs + 1):
        ms, zs = chunk(c)
        left(got_c.at[:, ms, zs], send_g.at[0, c], grp, trk)
        there, ms, zs = y_first(c)
        if there:
            left(got_y.at[: ny - 1, ms, zs], send_g.at[1, c], grp, trk)
            left(got_x.at[: NX - 1, ms, zs], send_g.at[3, c], grp, trk)
        ms, zs = x_first(c)
        left(got_xf.at[: NX - 1, :, ms, zs], send_g.at[2, c], grp, trk)
        left(got_yl.at[: ny - 1, ms, zs], send_g.at[4, c], grp, trk)
    left(got_z.at[: NZ - 1], send_g.at[5, 0], grp, trk)
    left(sum_c.at[0], send_s.at[0], grp, trk)
    left(sum_y.at[: ny - 1], send_s.at[1], grp, trk)
    left(sum_x.at[: NX - 1], send_s.at[2], grp, trk)
    left(sum_z.at[: NZ - 1], send_s.at[3], grp, trk)


def layer_back(fields, upstream, w_tile, gain):
    tracks, cells, width = fields.shape
    outs = w_tile.shape[1]
    length = tracks * cells
    ny = NYL * NYH
    any_, vmem = pl.BlockSpec(memory_space=pl.ANY), pl.BlockSpec(memory_space=pltpu.VMEM)
    dma = pltpu.SemaphoreType.DMA
    square = pltpu.VMEM((length, width), BF16)
    row = pltpu.VMEM((tracks, cells, width), BF16)
    return pl.pallas_call(
        row_kernel,
        out_shape=(
            jax.ShapeDtypeStruct((tracks, cells, width), BF16),
            jax.ShapeDtypeStruct((4, outs, 128), F32),
            jax.ShapeDtypeStruct((1, width), F32),
        ),
        in_specs=[any_, any_, any_, vmem],
        out_specs=[any_, vmem, vmem],
        scratch_shapes=[
            row,
            row,
            row,
            row,
            pltpu.VMEM((4, NZ, NX, NYH, outs, width), BF16),
            pltpu.VMEM((4, width, width), BF16),
            pltpu.VMEM((length, width), F32),
            pltpu.VMEM((length, 1), F32),
            pltpu.VMEM((width // HEAD, 2, length, length // 2), F32),
        ]
        + [square] * 10
        + [
            row,
            pltpu.VMEM((4, NZ, NX, NYH, outs, width), BF16),
            pltpu.VMEM((NYL, 4, NZ, NX, NYH, outs, 128), BF16),
            pltpu.VMEM((NYL, 4, NZ, NX, NYH, outs, 128), BF16),
            pltpu.VMEM((ny, 4, NZ, NX, outs, 128), BF16),
            pltpu.VMEM((4, NZ, NX, outs, 128), BF16),
            pltpu.VMEM((NX, 4, NZ, outs, 128), BF16),
            pltpu.VMEM((NX, NYL, 4, NZ, NYH, outs, 128), BF16),
            pltpu.VMEM((NYL, 4, NZ, NYH, outs, 128), BF16),
            pltpu.VMEM((ny, 4, NZ, outs, 128), BF16),
            pltpu.VMEM((4, NZ, outs, 128), BF16),
            pltpu.VMEM((NZ, 4, outs, 128), BF16),
            pltpu.VMEM((NC, 1, width), F32),
            pltpu.VMEM((ny, 1, width), F32),
            pltpu.VMEM((NX, 1, width), F32),
            pltpu.VMEM((NZ, 1, width), F32),
            dma((5,)),
            dma((3,)),
            dma((3,)),
            dma((11,)),
            dma((11,)),
            dma((6, 5)),
            dma((6, 5)),
            dma((4,)),
            dma((4,)),
        ],
        compiler_params=pltpu.CompilerParams(
            collective_id=1, has_side_effects=True, vmem_limit_bytes=56 << 20
        ),
        name="layer_back",
    )(fields, upstream, w_tile, gain)


def shards(fields, upstream, ln_gain, weights):
    tracks, cells, width = fields.shape
    w_tile = jnp.swapaxes(weights, 1, 2)
    grad_fields, grad_tile, grad_gain = layer_back(
        fields, upstream, w_tile, ln_gain.reshape(1, width)
    )
    return grad_fields, jnp.swapaxes(grad_tile, 1, 2), grad_gain.reshape(width)


def solution(mesh):
    in_specs = (P("grp", "trk", None), P("grp", "trk", None), P(), P(None, "grp", "trk"))
    out_specs = (P("grp", "trk", None), P(None, "grp", "trk"), P())
    return jax.shard_map(shards, mesh=mesh, in_specs=in_specs, out_specs=out_specs, check_vma=False)
```

```python
import jax
import jax.numpy as jnp
from jax import lax
from jax.experimental import pallas as pl
from jax.experimental.pallas import tpu as pltpu
from jax.sharding import PartitionSpec as P

NZ, NX, NYH = 8, 4, 2
NYL, NC = 2, 2
HEAD = 64
MESH = pl.DeviceIdType.MESH
F32, BF16 = jnp.float32, jnp.bfloat16


def dot(a, b, ca, cb):
    return lax.dot_general(a, b, (((ca,), (cb,)), ((), ())), preferred_element_type=F32)


def position():
    grp, trk = lax.axis_index("grp"), lax.axis_index("trk")
    z, x, y_hi = trk // (NX * NYH), (trk // NYH) % NX, trk % NYH
    y_lo, core = grp // NC, grp % NC
    return grp, trk, z, x, y_hi, y_lo, core


def trk_of(z, x, y_hi):
    return (z * NX + x) * NYH + y_hi


def remote(src, dst, send, recv, grp, trk):
    return pltpu.make_async_remote_copy(
        src_ref=src, dst_ref=dst, send_sem=send, recv_sem=recv,
        device_id=(grp, trk), device_id_type=MESH,
    )


def landed(view, recv, grp, trk):
    remote(view, view, recv, recv, grp, trk).wait_recv()


def left(view, send, grp, trk):
    remote(view, view, send, send, grp, trk).wait_send()


def lanes(grp):
    return pl.ds(pl.multiple_of(grp * 128, 128), 128)


def flips(value, count, stride):
    bits = count.bit_length() - 1
    return [(1 - 2 * ((value // 2**b) % 2)) * (2**b * stride) for b in range(bits)]


def row_kernel(
    f_ref, u_ref, w_ref, gain_ref, out_ref, gw_ref, gg_ref,
    fs, us, fr, ur, wf, wt, cen_ref, inv_ref, prob_ref,
    up, nor, qr, kr, vr, gar, atr, gqr, gkr, gvr, branch,
    raw, got_c, acc_c, got_y, acc_y, got_x, got_xf, acc_xf, got_yl, acc, got_z,
    sum_c, sum_y, sum_x, sum_z,
    local, send_a, recv_a, send_w, recv_w, send_g, recv_g, send_s, recv_s,
):
    grp, trk, z, x, y_hi, y_lo, core = position()
    tracks, cells, width = f_ref.shape
    length = tracks * cells
    plane = NX * NYH
    ny = NYL * NYH
    y_at = y_hi * NYL + y_lo
    sibling = y_lo * NC + 1 - core

    def y_peer(s):
        return (y_lo + s % 2) % NYL, (y_hi + s // 2) % NYH

    z_peers = [(grp, trk_of((z + s) % NZ, x, y_hi)) for s in range(1, NZ)]
    x_peers = [(grp, trk_of(z, (x + s) % NX, y_hi)) for s in range(1, NX)]
    y_peers = []
    for s in range(1, ny):
        low, high = y_peer(s)
        y_peers.append((low * NC + core, trk_of(z, x, high)))

    loads = [
        pltpu.make_async_copy(src, dst, local.at[3 + i])
        for i, (src, dst) in enumerate(((f_ref, fs), (u_ref, us)))
    ]
    for load in loads:
        load.start()
    mine = wf.at[:, z, x, y_hi, :, lanes(grp)]
    own = pltpu.make_async_copy(w_ref, mine, local.at[2])
    own.start()

    barrier = pltpu.get_barrier_semaphore()

    def greet(step, carry):
        to = lax.rem(trk + tracks // 2 + step, tracks)
        pl.semaphore_signal(barrier, inc=1, device_id=(grp, to), device_id_type=MESH)
        return carry

    lax.fori_loop(0, tracks // 2, greet, 0)
    lax.fori_loop(tracks // 2 + 1, tracks, greet, 0)
    for peer in y_peers:
        pl.semaphore_signal(barrier, inc=1, device_id=peer, device_id_type=MESH)
    pl.semaphore_signal(barrier, inc=1, device_id=(sibling, trk), device_id_type=MESH)
    pl.semaphore_wait(barrier, tracks - 1 + len(y_peers) + 1)

    for peer in z_peers:
        remote(w_ref, mine, send_w.at[0], recv_w.at[0], *peer).start()
    for load in loads:
        load.wait()

    in_plane = flips(trk % plane, plane, 1)
    over_z = flips(z, NZ, plane)
    offsets = []
    for k in range(plane):
        offset = trk * 0
        for b, flip in enumerate(in_plane):
            if (k >> b) & 1:
                offset = offset + flip
        offsets.append(offset)

    def exchange(src, dst, at, first, last):
        def some(high, skip):
            base = trk
            for b, flip in enumerate(over_z):
                base = base + ((high // 2**b) % 2) * flip
            for k in range(skip, plane):
                to = base + offsets[k]
                remote(src.at[to], dst.at[trk], send_a.at[at], recv_a.at[at], grp, to).start()

        def step(high, carry):
            some(high, 0)
            return carry

        if first == 0:
            pltpu.make_async_copy(src.at[trk], dst.at[trk], local.at[min(at, 1)]).start()
            some(0, 1)
            first = 1
        lax.fori_loop(first, last, step, 0)

    def exchanged(src, dst, at):
        landed(dst.at[: tracks - 1], recv_a.at[at], grp, trk)
        pltpu.make_async_copy(src.at[trk], dst.at[trk], local.at[min(at, 1)]).wait()

    exchange(fs, fr, 0, 0, NZ)
    own.wait()
    landed(wf.at[:, : NZ - 1, 0, 0, :, :128], recv_w.at[0], grp, trk)
    by_x = wf.at[:2, :, x, y_hi, :, lanes(grp)]
    by_y = wf.at[2:, :, x, y_hi, :, lanes(grp)]
    for peer in x_peers:
        remote(by_x, by_x, send_w.at[1], recv_w.at[1], *peer).start()
    for peer in y_peers:
        remote(by_y, by_y, send_w.at[10], recv_w.at[10], *peer).start()
    exchange(us, ur, 1, 0, NZ // 2)
    landed(wf.at[:2, :, : NX - 1, 0, :, :128], recv_w.at[1], grp, trk)
    landed(wf.at[2:, :, 0, 0, :, : (ny - 1) * 128], recv_w.at[10], grp, trk)
    for m in (0, 2, 1, 3):
        if m < 2:
            part = wf.at[m, :, :, y_hi, :, lanes(grp)]
            for peer in y_peers:
                remote(part, part, send_w.at[2 + m], recv_w.at[2 + m], *peer).start()
        else:
            for s in range(ny):
                low, high = y_peer(s)
                part = wf.at[m, :, x, high, :, lanes(low * NC + core)]
                for peer in x_peers:
                    remote(part, part, send_w.at[2 + m], recv_w.at[2 + m], *peer).start()
    exchange(us, ur, 1, NZ // 2, NZ)

    def last_stage(m):
        if m < 2:
            return wf.at[m, :, :, 0, :, : (ny - 1) * 128]
        return wf.at[m, :, : NX - 1, :, :, : ny // NYH * 128]

    def swap_weights(m):
        landed(last_stage(m), recv_w.at[2 + m], grp, trk)
        for low in range(NYL):
            half = wf.at[m, :, :, :, :, lanes(low * NC + core)]
            remote(half, half, send_w.at[6 + m], recv_w.at[6 + m], sibling, trk).start()

    def take_weights(m):
        landed(wf.at[m, :, :, :, :, : NYL * 128], recv_w.at[6 + m], grp, trk)
        wt[m] = wf[m].astype(F32).reshape(width, width).astype(BF16)

    for m in (0, 2, 1, 3):
        swap_weights(m)

    gain = gain_ref[...]
    exchanged(fs, fr, 0)
    values = fr[...].astype(F32).reshape(length, width)
    offset = values - jnp.mean(values, -1, keepdims=True)
    inv_std = lax.rsqrt(jnp.mean(offset * offset, -1, keepdims=True) + 1e-05)
    centred = offset * inv_std
    cen_ref[...] = centred
    inv_ref[...] = inv_std
    nor[...] = (centred * gain).astype(BF16)
    scaling = jnp.asarray(HEAD ** (-0.5), BF16)
    for m, ref in ((0, qr), (2, vr), (1, kr)):
        take_weights(m)
        ref[...] = dot(nor[...], wt[m], 1, 1).astype(BF16)
    half = length // 2
    lane = lax.broadcasted_iota(jnp.int32, (1, 128), 1)
    masks = [((lane >= h * HEAD) & (lane < (h + 1) * HEAD)).astype(BF16) for h in range(2)]
    pairs = width // 128

    def forward(pair, carry):
        cols = lanes(pair)
        q, k, v = qr[:, cols] * scaling, kr[:, cols], vr[:, cols]
        for part in range(2):
            rows = slice(part * half, (part + 1) * half)
            sum_o = jnp.zeros((half, 128), F32)
            for h in range(2):
                scores = dot(k * masks[h], q[rows], 1, 1)
                shifted = jnp.exp(scores - jnp.max(scores, 0, keepdims=True))
                prob = shifted * (1.0 / jnp.sum(shifted, 0, keepdims=True))
                prob_ref[2 * pair + h, part] = prob
                sum_o += dot(prob.astype(BF16), v * masks[h], 0, 0)
            atr[rows, cols] = sum_o.astype(BF16)
        return carry

    lax.fori_loop(0, pairs, forward, 0)

    def chunk(c):
        if c == 0:
            return slice(3, 4), slice(0, NZ)
        return slice(0, 3), slice((c - 1) * NZ // pairs, c * NZ // pairs)

    def y_first(c):
        return c > 0, slice(0, 2), chunk(c)[1]

    def x_first(c):
        return slice(2, 3) if c > 0 else slice(3, 4), chunk(c)[1]

    def core_start(c):
        ms, zs = chunk(c)
        for low in range(NYL):
            theirs = raw.at[ms, zs, :, :, :, lanes(low * NC + 1 - core)]
            remote(
                theirs, got_c.at[low, ms, zs], send_g.at[0, c], recv_g.at[0, c], sibling, trk
            ).start()

    def core_finish(c):
        ms, zs = chunk(c)
        landed(got_c.at[:, ms, zs], recv_g.at[0, c], grp, trk)
        for low in range(NYL):
            acc_c[low, ms, zs] = (
                raw[ms, zs, :, :, :, lanes(low * NC + core)].astype(F32)
                + got_c[low, ms, zs].astype(F32)
            ).astype(BF16)
        there, ms, zs = y_first(c)
        if there:
            for s in range(1, ny):
                low, high = y_peer(s)
                remote(
                    acc_c.at[low, ms, zs, :, high], got_y.at[y_at, ms, zs],
                    send_g.at[1, c], recv_g.at[1, c], *y_peers[s - 1],
                ).start()
        ms, zs = x_first(c)
        for s in range(1, NX):
            remote(
                acc_c.at[:, ms, zs, (x + s) % NX], got_xf.at[x, :, ms, zs],
                send_g.at[2, c], recv_g.at[2, c], *x_peers[s - 1],
            ).start()

    def second_start(c):
        there, ms, zs = y_first(c)
        if there:
            landed(got_y.at[: ny - 1, ms, zs], recv_g.at[1, c], grp, trk)
            total = acc_c[y_lo, ms, zs, :, y_hi].astype(F32)
            for s in range(1, ny):
                low, high = y_peer(s)
                total += got_y[high * NYL + low, ms, zs].astype(F32)
            acc_y[ms, zs] = total.astype(BF16)
            for s in range(1, NX):
                remote(
                    acc_y.at[ms, zs, (x + s) % NX], got_x.at[x, ms, zs],
                    send_g.at[3, c], recv_g.at[3, c], *x_peers[s - 1],
                ).start()
        ms, zs = x_first(c)
        landed(got_xf.at[: NX - 1, :, ms, zs], recv_g.at[2, c], grp, trk)
        total = acc_c[:, ms, zs, x].astype(F32)
        for s in range(1, NX):
            total += got_xf[(x + s) % NX, :, ms, zs].astype(F32)
        acc_xf[:, ms, zs] = total.astype(BF16)
        for s in range(1, ny):
            low, high = y_peer(s)
            remote(
                acc_xf.at[low, ms, zs, high], got_yl.at[y_at, ms, zs],
                send_g.at[4, c], recv_g.at[4, c], *y_peers[s - 1],
            ).start()

    def second_finish(c):
        there, ms, zs = y_first(c)
        if there:
            landed(got_x.at[: NX - 1, ms, zs], recv_g.at[3, c], grp, trk)
            total = acc_y[ms, zs, x].astype(F32)
            for s in range(1, NX):
                total += got_x[(x + s) % NX, ms, zs].astype(F32)
            acc[ms, zs] = total.astype(BF16)
        ms, zs = x_first(c)
        landed(got_yl.at[: ny - 1, ms, zs], recv_g.at[4, c], grp, trk)
        total = acc_xf[y_lo, ms, zs, y_hi].astype(F32)
        for s in range(1, ny):
            low, high = y_peer(s)
            total += got_yl[high * NYL + low, ms, zs].astype(F32)
        acc[ms, zs] = total.astype(BF16)

    raw_tiles = raw.shape[2:]

    exchanged(us, ur, 1)
    up[...] = ur[...].astype(F32).reshape(length, width).astype(BF16)
    take_weights(3)
    gar[...] = dot(up[...], wt[3], 1, 0).astype(BF16)
    raw[3] = dot(up[...], atr[...], 0, 0).reshape(raw.shape[1:]).astype(BF16)
    core_start(0)
    for pair in range(pairs):
        cols = slice(pair * 128, (pair + 1) * 128)
        q, k, v, ga = qr[:, cols], kr[:, cols], vr[:, cols], gar[:, cols]
        scaled_ga = ga * scaling
        sum_k = jnp.zeros((length, 128), F32)
        sum_v = jnp.zeros((length, 128), F32)
        for part in range(2):
            rows = slice(part * half, (part + 1) * half)
            sum_q = jnp.zeros((half, 128), F32)
            for h in range(2):
                prob = prob_ref[2 * pair + h, part]
                dprobs = dot(v * masks[h], scaled_ga[rows], 1, 1)
                row_dot = jnp.sum(prob * dprobs, 0, keepdims=True)
                grad = (prob * (dprobs - row_dot)).astype(BF16)
                sum_q += dot(grad, k * masks[h], 0, 0)
                sum_v += dot(prob.astype(BF16), ga[rows] * masks[h], 1, 0)
                sum_k += dot(grad, q[rows] * masks[h], 1, 0)
            gqr[rows, cols] = sum_q.astype(BF16)
        gkr[:, cols] = sum_k.astype(BF16)
        gvr[:, cols] = sum_v.astype(BF16)
        zs = chunk(pair + 1)[1]
        for m, ref in enumerate((gqr, gkr, gvr)):
            piece = dot(ref[:, cols], nor[...], 0, 0)
            raw[m, zs] = piece.reshape((zs.stop - zs.start,) + raw_tiles).astype(BF16)
        core_start(pair + 1)
        core_finish(pair)
        if pair >= 2:
            second_start(pair - 2)
    grad_normed = (
        dot(gqr[...], wt[0], 1, 0) + dot(gkr[...], wt[1], 1, 0) + dot(gvr[...], wt[2], 1, 0)
    )
    centred = cen_ref[...]
    sum_c[core] = jnp.sum(grad_normed * centred, 0, keepdims=True)
    remote(sum_c.at[core], sum_c.at[core], send_s.at[0], recv_s.at[0], sibling, trk).start()
    core_finish(pairs)
    second_start(pairs - 2)
    landed(sum_c.at[0], recv_s.at[0], grp, trk)
    sum_y[y_at] = sum_c[0] + sum_c[1]
    for peer in y_peers:
        remote(sum_y.at[y_at], sum_y.at[y_at], send_s.at[1], recv_s.at[1], *peer).start()
    scaled = grad_normed * gain
    grad = inv_ref[...] * (
        scaled
        - jnp.mean(scaled, -1, keepdims=True)
        - centred * jnp.mean(scaled * centred, -1, keepdims=True)
    )
    grad = up[...].astype(F32) + grad.astype(BF16).astype(F32)
    branch[...] = grad.reshape(tracks, cells, width).astype(BF16)
    exchange(branch, out_ref, 2, 0, NZ * 3 // 8)
    second_start(pairs - 1)
    landed(sum_y.at[: ny - 1], recv_s.at[1], grp, trk)
    all_y = sum_y[0]
    for s in range(1, ny):
        all_y += sum_y[s]
    sum_x[x] = all_y
    for peer in x_peers:
        remote(sum_x.at[x], sum_x.at[x], send_s.at[2], recv_s.at[2], *peer).start()
    second_start(pairs)
    exchange(branch, out_ref, 2, NZ * 3 // 8, NZ * 6 // 8)
    for c in range(pairs + 1):
        second_finish(c)
    for s in range(1, NZ):
        remote(
            acc.at[:, (z + s) % NZ], got_z.at[z], send_g.at[5, 0], recv_g.at[5, 0],
            *z_peers[s - 1],
        ).start()
    landed(sum_x.at[: NX - 1], recv_s.at[2], grp, trk)
    all_x = sum_x[0]
    for s in range(1, NX):
        all_x += sum_x[s]
    sum_z[z] = all_x
    for peer in z_peers:
        remote(sum_z.at[z], sum_z.at[z], send_s.at[3], recv_s.at[3], *peer).start()
    exchange(branch, out_ref, 2, NZ * 6 // 8, NZ)
    landed(got_z.at[: NZ - 1], recv_g.at[5, 0], grp, trk)
    total = acc[:, z].astype(F32)
    for s in range(1, NZ):
        total += got_z[(z + s) % NZ].astype(F32)
    factor = float(length * lax.axis_size("grp") * tracks) ** (-0.5)
    gw_ref[...] = total * factor
    landed(sum_z.at[: NZ - 1], recv_s.at[3], grp, trk)
    all_z = sum_z[0]
    for s in range(1, NZ):
        all_z += sum_z[s]
    gg_ref[...] = all_z * factor
    exchanged(branch, out_ref, 2)

    for at in range(3):
        left(out_ref.at[: tracks - 1], send_a.at[at], grp, trk)
    left(wf.at[:, : NZ - 1, 0, 0, :, :128], send_w.at[0], grp, trk)
    left(wf.at[:2, :, : NX - 1, 0, :, :128], send_w.at[1], grp, trk)
    left(wf.at[2:, :, 0, 0, :, : (ny - 1) * 128], send_w.at[10], grp, trk)
    for m in range(4):
        left(last_stage(m), send_w.at[2 + m], grp, trk)
        left(wf.at[m, :, :, :, :, : NYL * 128], send_w.at[6 + m], grp, trk)
    for c in range(pairs + 1):
        ms, zs = chunk(c)
        left(got_c.at[:, ms, zs], send_g.at[0, c], grp, trk)
        there, ms, zs = y_first(c)
        if there:
            left(got_y.at[: ny - 1, ms, zs], send_g.at[1, c], grp, trk)
            left(got_x.at[: NX - 1, ms, zs], send_g.at[3, c], grp, trk)
        ms, zs = x_first(c)
        left(got_xf.at[: NX - 1, :, ms, zs], send_g.at[2, c], grp, trk)
        left(got_yl.at[: ny - 1, ms, zs], send_g.at[4, c], grp, trk)
    left(got_z.at[: NZ - 1], send_g.at[5, 0], grp, trk)
    left(sum_c.at[0], send_s.at[0], grp, trk)
    left(sum_y.at[: ny - 1], send_s.at[1], grp, trk)
    left(sum_x.at[: NX - 1], send_s.at[2], grp, trk)
    left(sum_z.at[: NZ - 1], send_s.at[3], grp, trk)


def layer_back(fields, upstream, w_tile, gain):
    tracks, cells, width = fields.shape
    outs = w_tile.shape[1]
    length = tracks * cells
    ny = NYL * NYH
    any_, vmem = pl.BlockSpec(memory_space=pl.ANY), pl.BlockSpec(memory_space=pltpu.VMEM)
    dma = pltpu.SemaphoreType.DMA
    square = pltpu.VMEM((length, width), BF16)
    row = pltpu.VMEM((tracks, cells, width), BF16)
    return pl.pallas_call(
        row_kernel,
        out_shape=(
            jax.ShapeDtypeStruct((tracks, cells, width), BF16),
            jax.ShapeDtypeStruct((4, outs, 128), F32),
            jax.ShapeDtypeStruct((1, width), F32),
        ),
        in_specs=[any_, any_, any_, vmem],
        out_specs=[any_, vmem, vmem],
        scratch_shapes=[
            row,
            row,
            row,
            row,
            pltpu.VMEM((4, NZ, NX, NYH, outs, width), BF16),
            pltpu.VMEM((4, width, width), BF16),
            pltpu.VMEM((length, width), F32),
            pltpu.VMEM((length, 1), F32),
            pltpu.VMEM((width // HEAD, 2, length, length // 2), F32),
        ]
        + [square] * 10
        + [
            row,
            pltpu.VMEM((4, NZ, NX, NYH, outs, width), BF16),
            pltpu.VMEM((NYL, 4, NZ, NX, NYH, outs, 128), BF16),
            pltpu.VMEM((NYL, 4, NZ, NX, NYH, outs, 128), BF16),
            pltpu.VMEM((ny, 4, NZ, NX, outs, 128), BF16),
            pltpu.VMEM((4, NZ, NX, outs, 128), BF16),
            pltpu.VMEM((NX, 4, NZ, outs, 128), BF16),
            pltpu.VMEM((NX, NYL, 4, NZ, NYH, outs, 128), BF16),
            pltpu.VMEM((NYL, 4, NZ, NYH, outs, 128), BF16),
            pltpu.VMEM((ny, 4, NZ, outs, 128), BF16),
            pltpu.VMEM((4, NZ, outs, 128), BF16),
            pltpu.VMEM((NZ, 4, outs, 128), BF16),
            pltpu.VMEM((NC, 1, width), F32),
            pltpu.VMEM((ny, 1, width), F32),
            pltpu.VMEM((NX, 1, width), F32),
            pltpu.VMEM((NZ, 1, width), F32),
            dma((5,)),
            dma((3,)),
            dma((3,)),
            dma((11,)),
            dma((11,)),
            dma((6, 5)),
            dma((6, 5)),
            dma((4,)),
            dma((4,)),
        ],
        compiler_params=pltpu.CompilerParams(
            collective_id=1, has_side_effects=True, vmem_limit_bytes=56 << 20
        ),
        name="layer_back",
    )(fields, upstream, w_tile, gain)


def shards(fields, upstream, ln_gain, weights):
    tracks, cells, width = fields.shape
    w_tile = jnp.swapaxes(weights, 1, 2)
    grad_fields, grad_tile, grad_gain = layer_back(
        fields, upstream, w_tile, ln_gain.reshape(1, width)
    )
    return grad_fields, jnp.swapaxes(grad_tile, 1, 2), grad_gain.reshape(width)


def solution(mesh):
    in_specs = (P("grp", "trk", None), P("grp", "trk", None), P(), P(None, "grp", "trk"))
    out_specs = (P("grp", "trk", None), P(None, "grp", "trk"), P())
    return jax.shard_map(shards, mesh=mesh, in_specs=in_specs, out_specs=out_specs, check_vma=False)
```

```python
import jax
import jax.numpy as jnp
from jax import lax
from jax.experimental import pallas as pl
from jax.experimental.pallas import tpu as pltpu
from jax.sharding import PartitionSpec as P

NZ, NX, NYH = 8, 4, 2
NYL, NC = 2, 2
HEAD = 64
MESH = pl.DeviceIdType.MESH
F32, BF16 = jnp.float32, jnp.bfloat16


def dot(a, b, ca, cb):
    return lax.dot_general(a, b, (((ca,), (cb,)), ((), ())), preferred_element_type=F32)


def position():
    grp, trk = lax.axis_index("grp"), lax.axis_index("trk")
    z, x, y_hi = trk // (NX * NYH), (trk // NYH) % NX, trk % NYH
    y_lo, core = grp // NC, grp % NC
    return grp, trk, z, x, y_hi, y_lo, core


def trk_of(z, x, y_hi):
    return (z * NX + x) * NYH + y_hi


def remote(src, dst, send, recv, grp, trk):
    return pltpu.make_async_remote_copy(
        src_ref=src, dst_ref=dst, send_sem=send, recv_sem=recv,
        device_id=(grp, trk), device_id_type=MESH,
    )


def landed(view, recv, grp, trk):
    remote(view, view, recv, recv, grp, trk).wait_recv()


def left(view, send, grp, trk):
    remote(view, view, send, send, grp, trk).wait_send()


def lanes(grp):
    return pl.ds(pl.multiple_of(grp * 128, 128), 128)


def flips(value, count, stride):
    bits = count.bit_length() - 1
    return [(1 - 2 * ((value // 2**b) % 2)) * (2**b * stride) for b in range(bits)]


def row_kernel(
    f_ref, u_ref, w_ref, gain_ref, out_ref, gw_ref, gg_ref,
    fs, us, fr, ur, wf, wt, cen_ref, inv_ref, prob_ref,
    up, nor, qr, kr, vr, gar, atr, gqr, gkr, gvr, branch,
    raw, got_c, acc_c, got_y, acc_y, got_x, got_xf, acc_xf, got_yl, got_d, acc, got_z,
    sum_c, sum_y, sum_z,
    local, send_a, recv_a, send_w, recv_w, send_g, recv_g, send_s, recv_s,
):
    grp, trk, z, x, y_hi, y_lo, core = position()
    tracks, cells, width = f_ref.shape
    length = tracks * cells
    plane = NX * NYH
    ny = NYL * NYH
    y_at = y_hi * NYL + y_lo
    sibling = y_lo * NC + 1 - core

    def y_peer(s):
        return (y_lo + s % 2) % NYL, (y_hi + s // 2) % NYH

    z_peers = [(grp, trk_of((z + s) % NZ, x, y_hi)) for s in range(1, NZ)]
    x_peers = [(grp, trk_of(z, (x + s) % NX, y_hi)) for s in range(1, NX)]
    y_peers = []
    for s in range(1, ny):
        low, high = y_peer(s)
        y_peers.append((low * NC + core, trk_of(z, x, high)))

    xy_at = y_at * NX + x
    plane_peers = []
    for s in range(ny):
        low, high = y_peer(s)
        for far in range(NX):
            if s + far > 0:
                at_x = (x + far) % NX
                plane_peers.append((low, high, at_x, (low * NC + core, trk_of(z, at_x, high))))

    loads = [
        pltpu.make_async_copy(src, dst, local.at[3 + i])
        for i, (src, dst) in enumerate(((f_ref, fs), (u_ref, us)))
    ]
    for load in loads:
        load.start()
    mine = wf.at[:, z, x, y_hi, :, lanes(grp)]
    own = pltpu.make_async_copy(w_ref, mine, local.at[2])
    own.start()

    barrier = pltpu.get_barrier_semaphore()

    def greet(step, carry):
        to = lax.rem(trk + tracks // 2 + step, tracks)
        pl.semaphore_signal(barrier, inc=1, device_id=(grp, to), device_id_type=MESH)
        return carry

    lax.fori_loop(0, tracks // 2, greet, 0)
    lax.fori_loop(tracks // 2 + 1, tracks, greet, 0)
    for k in range(plane):
        to = ((1 - y_lo) * NC + core, z * plane + k)
        pl.semaphore_signal(barrier, inc=1, device_id=to, device_id_type=MESH)
    pl.semaphore_signal(barrier, inc=1, device_id=(sibling, trk), device_id_type=MESH)
    pl.semaphore_wait(barrier, tracks - 1 + plane + 1)

    for peer in z_peers:
        remote(w_ref, mine, send_w.at[0], recv_w.at[0], *peer).start()
    for load in loads:
        load.wait()

    in_plane = flips(trk % plane, plane, 1)
    over_z = flips(z, NZ, plane)
    offsets = []
    for k in range(plane):
        offset = trk * 0
        for b, flip in enumerate(in_plane):
            if (k >> b) & 1:
                offset = offset + flip
        offsets.append(offset)

    def exchange(src, dst, at, first, last):
        def some(high, skip):
            base = trk
            for b, flip in enumerate(over_z):
                base = base + ((high // 2**b) % 2) * flip
            for k in range(skip, plane):
                to = base + offsets[k]
                remote(src.at[to], dst.at[trk], send_a.at[at], recv_a.at[at], grp, to).start()

        def step(high, carry):
            some(high, 0)
            return carry

        if first == 0:
            pltpu.make_async_copy(src.at[trk], dst.at[trk], local.at[min(at, 1)]).start()
            some(0, 1)
            first = 1
        lax.fori_loop(first, last, step, 0)

    def exchanged(src, dst, at):
        landed(dst.at[: tracks - 1], recv_a.at[at], grp, trk)
        pltpu.make_async_copy(src.at[trk], dst.at[trk], local.at[min(at, 1)]).wait()

    exchange(fs, fr, 0, 0, NZ)
    own.wait()
    landed(wf.at[:, : NZ - 1, 0, 0, :, :128], recv_w.at[0], grp, trk)
    by_x = wf.at[:2, :, x, y_hi, :, lanes(grp)]
    by_y = wf.at[2:, :, x, y_hi, :, lanes(grp)]
    for peer in x_peers:
        remote(by_x, by_x, send_w.at[1], recv_w.at[1], *peer).start()
    for peer in y_peers:
        remote(by_y, by_y, send_w.at[10], recv_w.at[10], *peer).start()
    exchange(us, ur, 1, 0, NZ // 2)
    landed(wf.at[:2, :, : NX - 1, 0, :, :128], recv_w.at[1], grp, trk)
    landed(wf.at[2:, :, 0, 0, :, : (ny - 1) * 128], recv_w.at[10], grp, trk)
    for m in (0, 2, 1, 3):
        if m < 2:
            part = wf.at[m, :, :, y_hi, :, lanes(grp)]
            for peer in y_peers:
                remote(part, part, send_w.at[2 + m], recv_w.at[2 + m], *peer).start()
        else:
            for s in range(ny):
                low, high = y_peer(s)
                part = wf.at[m, :, x, high, :, lanes(low * NC + core)]
                for peer in x_peers:
                    remote(part, part, send_w.at[2 + m], recv_w.at[2 + m], *peer).start()
    exchange(us, ur, 1, NZ // 2, NZ)

    def last_stage(m):
        if m < 2:
            return wf.at[m, :, :, 0, :, : (ny - 1) * 128]
        return wf.at[m, :, : NX - 1, :, :, : ny // NYH * 128]

    def swap_weights(m):
        landed(last_stage(m), recv_w.at[2 + m], grp, trk)
        for low in range(NYL):
            half = wf.at[m, :, :, :, :, lanes(low * NC + core)]
            remote(half, half, send_w.at[6 + m], recv_w.at[6 + m], sibling, trk).start()

    def take_weights(m):
        landed(wf.at[m, :, :, :, :, : NYL * 128], recv_w.at[6 + m], grp, trk)
        wt[m] = wf[m].astype(F32).reshape(width, width).astype(BF16)

    for m in (0, 2, 1, 3):
        swap_weights(m)

    gain = gain_ref[...]
    exchanged(fs, fr, 0)
    values = fr[...].astype(F32).reshape(length, width)
    offset = values - jnp.mean(values, -1, keepdims=True)
    inv_std = lax.rsqrt(jnp.mean(offset * offset, -1, keepdims=True) + 1e-05)
    centred = offset * inv_std
    cen_ref[...] = centred
    inv_ref[...] = inv_std
    nor[...] = (centred * gain).astype(BF16)
    scaling = jnp.asarray(HEAD ** (-0.5), BF16)
    for m, ref in ((0, qr), (2, vr), (1, kr)):
        take_weights(m)
        ref[...] = dot(nor[...], wt[m], 1, 1).astype(BF16)
    half = length // 2
    lane = lax.broadcasted_iota(jnp.int32, (1, 128), 1)
    masks = [((lane >= h * HEAD) & (lane < (h + 1) * HEAD)).astype(BF16) for h in range(2)]
    turned = lax.broadcasted_iota(jnp.int32, (128, 1), 0)
    turned_masks = [
        ((turned >= h * HEAD) & (turned < (h + 1) * HEAD)).astype(BF16) for h in range(2)
    ]
    pairs = width // 128

    def forward(pair, carry):
        cols = lanes(pair)
        q, k, v = qr[:, cols] * scaling, kr[:, cols], vr[:, cols]
        v_turned = v.T
        k_of = [k * masks[h] for h in range(2)]
        v_of = [v_turned * turned_masks[h] for h in range(2)]
        for part in range(2):
            rows = slice(part * half, (part + 1) * half)
            sum_o = jnp.zeros((128, half), F32)
            for h in range(2):
                scores = dot(k_of[h], q[rows], 1, 1)
                shifted = jnp.exp(scores - jnp.max(scores, 0, keepdims=True))
                prob = shifted * (1.0 / jnp.sum(shifted, 0, keepdims=True))
                prob_ref[2 * pair + h, part] = prob
                sum_o += dot(v_of[h], prob.astype(BF16), 1, 0)
            atr[rows, cols] = sum_o.T.astype(BF16)
        return carry

    lax.fori_loop(0, pairs, forward, 0)

    def chunk(c):
        if c == 0:
            return slice(3, 4), slice(0, NZ)
        return slice(0, 3), slice((c - 1) * NZ // pairs, c * NZ // pairs)

    def y_first(c):
        return c > 0, slice(0, 2), chunk(c)[1]

    def x_first(c):
        return slice(2, 3) if c > 0 else slice(3, 4), chunk(c)[1]

    def core_start(c):
        ms, zs = chunk(c)
        for low in range(NYL):
            theirs = raw.at[ms, zs, :, :, :, lanes(low * NC + 1 - core)]
            remote(
                theirs, got_c.at[low, ms, zs], send_g.at[0, c], recv_g.at[0, c], sibling, trk
            ).start()

    def core_finish(c):
        ms, zs = chunk(c)
        landed(got_c.at[:, ms, zs], recv_g.at[0, c], grp, trk)
        for low in range(NYL):
            acc_c[low, ms, zs] = (
                raw[ms, zs, :, :, :, lanes(low * NC + core)].astype(F32)
                + got_c[low, ms, zs].astype(F32)
            ).astype(BF16)
        if c == pairs:
            for low, high, at_x, to in plane_peers:
                remote(
                    acc_c.at[low, ms, zs, at_x, high], got_d.at[xy_at],
                    send_g.at[1, c], recv_g.at[1, c], *to,
                ).start()
            return
        there, ms, zs = y_first(c)
        if there:
            for s in range(1, ny):
                low, high = y_peer(s)
                remote(
                    acc_c.at[low, ms, zs, :, high], got_y.at[y_at, ms, zs],
                    send_g.at[1, c], recv_g.at[1, c], *y_peers[s - 1],
                ).start()
        ms, zs = x_first(c)
        for s in range(1, NX):
            remote(
                acc_c.at[:, ms, zs, (x + s) % NX], got_xf.at[x, :, ms, zs],
                send_g.at[2, c], recv_g.at[2, c], *x_peers[s - 1],
            ).start()

    def second_start(c):
        there, ms, zs = y_first(c)
        if there:
            landed(got_y.at[: ny - 1, ms, zs], recv_g.at[1, c], grp, trk)
            total = acc_c[y_lo, ms, zs, :, y_hi].astype(F32)
            for s in range(1, ny):
                low, high = y_peer(s)
                total += got_y[high * NYL + low, ms, zs].astype(F32)
            acc_y[ms, zs] = total.astype(BF16)
            for s in range(1, NX):
                remote(
                    acc_y.at[ms, zs, (x + s) % NX], got_x.at[x, ms, zs],
                    send_g.at[3, c], recv_g.at[3, c], *x_peers[s - 1],
                ).start()
        ms, zs = x_first(c)
        landed(got_xf.at[: NX - 1, :, ms, zs], recv_g.at[2, c], grp, trk)
        total = acc_c[:, ms, zs, x].astype(F32)
        for s in range(1, NX):
            total += got_xf[(x + s) % NX, :, ms, zs].astype(F32)
        acc_xf[:, ms, zs] = total.astype(BF16)
        for s in range(1, ny):
            low, high = y_peer(s)
            remote(
                acc_xf.at[low, ms, zs, high], got_yl.at[y_at, ms, zs],
                send_g.at[4, c], recv_g.at[4, c], *y_peers[s - 1],
            ).start()

    def direct_finish(c):
        ms, zs = chunk(c)
        landed(got_d.at[: ny * NX - 1], recv_g.at[1, c], grp, trk)
        total = acc_c[y_lo, ms, zs, x, y_hi].astype(F32)
        for low, high, at_x, _ in plane_peers:
            total += got_d[(high * NYL + low) * NX + at_x].astype(F32)
        acc[ms, zs] = total.astype(BF16)

    def second_finish(c):
        there, ms, zs = y_first(c)
        if there:
            landed(got_x.at[: NX - 1, ms, zs], recv_g.at[3, c], grp, trk)
            total = acc_y[ms, zs, x].astype(F32)
            for s in range(1, NX):
                total += got_x[(x + s) % NX, ms, zs].astype(F32)
            acc[ms, zs] = total.astype(BF16)
        ms, zs = x_first(c)
        landed(got_yl.at[: ny - 1, ms, zs], recv_g.at[4, c], grp, trk)
        total = acc_xf[y_lo, ms, zs, y_hi].astype(F32)
        for s in range(1, ny):
            low, high = y_peer(s)
            total += got_yl[high * NYL + low, ms, zs].astype(F32)
        acc[ms, zs] = total.astype(BF16)

    raw_tiles = raw.shape[2:]

    exchanged(us, ur, 1)
    up[...] = ur[...].astype(F32).reshape(length, width).astype(BF16)
    take_weights(3)
    gar[...] = dot(up[...], wt[3], 1, 0).astype(BF16)
    raw[3] = dot(up[...], atr[...], 0, 0).reshape(raw.shape[1:]).astype(BF16)
    core_start(0)
    for pair in range(pairs):
        cols = slice(pair * 128, (pair + 1) * 128)
        q, k, v, ga = qr[:, cols], kr[:, cols], vr[:, cols], gar[:, cols]
        scaled_ga = ga * scaling
        k_turned = k.T
        k_of = [k_turned * turned_masks[h] for h in range(2)]
        v_of = [v * masks[h] for h in range(2)]
        q_of = [q * masks[h] for h in range(2)]
        ga_of = [ga * masks[h] for h in range(2)]
        sum_k = jnp.zeros((length, 128), F32)
        sum_v = jnp.zeros((length, 128), F32)
        for part in range(2):
            rows = slice(part * half, (part + 1) * half)
            sum_q = jnp.zeros((128, half), F32)
            for h in range(2):
                prob = prob_ref[2 * pair + h, part]
                dprobs = dot(v_of[h], scaled_ga[rows], 1, 1)
                row_dot = jnp.sum(prob * dprobs, 0, keepdims=True)
                grad = (prob * (dprobs - row_dot)).astype(BF16)
                sum_q += dot(k_of[h], grad, 1, 0)
                sum_v += dot(prob.astype(BF16), ga_of[h][rows], 1, 0)
                sum_k += dot(grad, q_of[h][rows], 1, 0)
            gqr[cols, rows] = sum_q.astype(BF16)
        gkr[:, cols] = sum_k.astype(BF16)
        gvr[:, cols] = sum_v.astype(BF16)
        zs = chunk(pair + 1)[1]
        for m, piece in enumerate((
            dot(gqr[cols, :], nor[...], 1, 0),
            dot(gkr[:, cols], nor[...], 0, 0),
            dot(gvr[:, cols], nor[...], 0, 0),
        )):
            raw[m, zs] = piece.reshape((zs.stop - zs.start,) + raw_tiles).astype(BF16)
        core_start(pair + 1)
        core_finish(pair)
        if pair >= 2:
            second_start(pair - 2)
    grad_normed = (
        dot(gqr[...], wt[0], 0, 0) + dot(gkr[...], wt[1], 1, 0) + dot(gvr[...], wt[2], 1, 0)
    )
    centred = cen_ref[...]
    sum_c[core] = jnp.sum(grad_normed * centred, 0, keepdims=True)
    remote(sum_c.at[core], sum_c.at[core], send_s.at[0], recv_s.at[0], sibling, trk).start()
    core_finish(pairs)
    landed(sum_c.at[0], recv_s.at[0], grp, trk)
    sum_y[xy_at] = sum_c[0] + sum_c[1]
    for _, _, _, to in plane_peers:
        remote(sum_y.at[xy_at], sum_y.at[xy_at], send_s.at[1], recv_s.at[1], *to).start()
    second_start(pairs - 2)
    scaled = grad_normed * gain
    grad = inv_ref[...] * (
        scaled
        - jnp.mean(scaled, -1, keepdims=True)
        - centred * jnp.mean(scaled * centred, -1, keepdims=True)
    )
    grad = up[...].astype(F32) + grad.astype(BF16).astype(F32)
    branch[...] = grad.reshape(tracks, cells, width).astype(BF16)
    second_start(pairs - 1)
    exchange(branch, out_ref, 2, 0, NZ * 5 // 8)
    direct_finish(pairs)
    for c in range(pairs):
        second_finish(c)
    for s in range(1, NZ):
        remote(
            acc.at[:, (z + s) % NZ], got_z.at[z], send_g.at[5, 0], recv_g.at[5, 0],
            *z_peers[s - 1],
        ).start()
    landed(sum_y.at[: ny * NX - 1], recv_s.at[1], grp, trk)
    all_y = sum_y[0]
    for s in range(1, ny * NX):
        all_y += sum_y[s]
    sum_z[z] = all_y
    for peer in z_peers:
        remote(sum_z.at[z], sum_z.at[z], send_s.at[3], recv_s.at[3], *peer).start()
    exchange(branch, out_ref, 2, NZ * 5 // 8, NZ)
    landed(got_z.at[: NZ - 1], recv_g.at[5, 0], grp, trk)
    total = acc[:, z].astype(F32)
    for s in range(1, NZ):
        total += got_z[(z + s) % NZ].astype(F32)
    factor = float(length * lax.axis_size("grp") * tracks) ** (-0.5)
    gw_ref[...] = total * factor
    landed(sum_z.at[: NZ - 1], recv_s.at[3], grp, trk)
    all_z = sum_z[0]
    for s in range(1, NZ):
        all_z += sum_z[s]
    gg_ref[...] = all_z * factor
    exchanged(branch, out_ref, 2)

    for at in range(3):
        left(out_ref.at[: tracks - 1], send_a.at[at], grp, trk)
    left(wf.at[:, : NZ - 1, 0, 0, :, :128], send_w.at[0], grp, trk)
    left(wf.at[:2, :, : NX - 1, 0, :, :128], send_w.at[1], grp, trk)
    left(wf.at[2:, :, 0, 0, :, : (ny - 1) * 128], send_w.at[10], grp, trk)
    for m in range(4):
        left(last_stage(m), send_w.at[2 + m], grp, trk)
        left(wf.at[m, :, :, :, :, : NYL * 128], send_w.at[6 + m], grp, trk)
    for c in range(pairs + 1):
        ms, zs = chunk(c)
        left(got_c.at[:, ms, zs], send_g.at[0, c], grp, trk)
        if c == pairs:
            left(got_d.at[: ny * NX - 1], send_g.at[1, c], grp, trk)
            break
        there, ms, zs = y_first(c)
        if there:
            left(got_y.at[: ny - 1, ms, zs], send_g.at[1, c], grp, trk)
            left(got_x.at[: NX - 1, ms, zs], send_g.at[3, c], grp, trk)
        ms, zs = x_first(c)
        left(got_xf.at[: NX - 1, :, ms, zs], send_g.at[2, c], grp, trk)
        left(got_yl.at[: ny - 1, ms, zs], send_g.at[4, c], grp, trk)
    left(got_z.at[: NZ - 1], send_g.at[5, 0], grp, trk)
    left(sum_c.at[0], send_s.at[0], grp, trk)
    left(sum_y.at[: ny * NX - 1], send_s.at[1], grp, trk)
    left(sum_z.at[: NZ - 1], send_s.at[3], grp, trk)


def layer_back(fields, upstream, w_tile, gain):
    tracks, cells, width = fields.shape
    outs = w_tile.shape[1]
    length = tracks * cells
    ny = NYL * NYH
    any_, vmem = pl.BlockSpec(memory_space=pl.ANY), pl.BlockSpec(memory_space=pltpu.VMEM)
    dma = pltpu.SemaphoreType.DMA
    square = pltpu.VMEM((length, width), BF16)
    row = pltpu.VMEM((tracks, cells, width), BF16)
    return pl.pallas_call(
        row_kernel,
        out_shape=(
            jax.ShapeDtypeStruct((tracks, cells, width), BF16),
            jax.ShapeDtypeStruct((4, outs, 128), F32),
            jax.ShapeDtypeStruct((1, width), F32),
        ),
        in_specs=[any_, any_, any_, vmem],
        out_specs=[any_, vmem, vmem],
        scratch_shapes=[
            row,
            row,
            row,
            row,
            pltpu.VMEM((4, NZ, NX, NYH, outs, width), BF16),
            pltpu.VMEM((4, width, width), BF16),
            pltpu.VMEM((length, width), F32),
            pltpu.VMEM((length, 1), F32),
            pltpu.VMEM((width // HEAD, 2, length, length // 2), F32),
        ]
        + [square] * 7
        + [pltpu.VMEM((width, length), BF16)]
        + [square] * 2
        + [
            row,
            pltpu.VMEM((4, NZ, NX, NYH, outs, width), BF16),
            pltpu.VMEM((NYL, 4, NZ, NX, NYH, outs, 128), BF16),
            pltpu.VMEM((NYL, 4, NZ, NX, NYH, outs, 128), BF16),
            pltpu.VMEM((ny, 4, NZ, NX, outs, 128), BF16),
            pltpu.VMEM((4, NZ, NX, outs, 128), BF16),
            pltpu.VMEM((NX, 4, NZ, outs, 128), BF16),
            pltpu.VMEM((NX, NYL, 4, NZ, NYH, outs, 128), BF16),
            pltpu.VMEM((NYL, 4, NZ, NYH, outs, 128), BF16),
            pltpu.VMEM((ny, 4, NZ, outs, 128), BF16),
            pltpu.VMEM((ny * NX, 3, NZ * 128 // width, outs, 128), BF16),
            pltpu.VMEM((4, NZ, outs, 128), BF16),
            pltpu.VMEM((NZ, 4, outs, 128), BF16),
            pltpu.VMEM((NC, 1, width), F32),
            pltpu.VMEM((ny * NX, 1, width), F32),
            pltpu.VMEM((NZ, 1, width), F32),
            dma((5,)),
            dma((3,)),
            dma((3,)),
            dma((11,)),
            dma((11,)),
            dma((6, 5)),
            dma((6, 5)),
            dma((4,)),
            dma((4,)),
        ],
        compiler_params=pltpu.CompilerParams(
            collective_id=1, has_side_effects=True, vmem_limit_bytes=56 << 20
        ),
        name="layer_back",
    )(fields, upstream, w_tile, gain)


def shards(fields, upstream, ln_gain, weights):
    tracks, cells, width = fields.shape
    w_tile = jnp.swapaxes(weights, 1, 2)
    grad_fields, grad_tile, grad_gain = layer_back(
        fields, upstream, w_tile, ln_gain.reshape(1, width)
    )
    return grad_fields, jnp.swapaxes(grad_tile, 1, 2), grad_gain.reshape(width)


def solution(mesh):
    in_specs = (P("grp", "trk", None), P("grp", "trk", None), P(), P(None, "grp", "trk"))
    out_specs = (P("grp", "trk", None), P(None, "grp", "trk"), P())
    return jax.shard_map(shards, mesh=mesh, in_specs=in_specs, out_specs=out_specs, check_vma=False)
```

```python
import jax
import jax.numpy as jnp
from jax import lax
from jax.experimental import pallas as pl
from jax.experimental.pallas import tpu as pltpu
from jax.sharding import PartitionSpec as P

NZ, NX, NYH = 8, 4, 2
NYL, NC = 2, 2
HEAD = 64
MESH = pl.DeviceIdType.MESH
F32, BF16 = jnp.float32, jnp.bfloat16


def dot(a, b, ca, cb):
    return lax.dot_general(a, b, (((ca,), (cb,)), ((), ())), preferred_element_type=F32)


def position():
    grp, trk = lax.axis_index("grp"), lax.axis_index("trk")
    z, x, y_hi = trk // (NX * NYH), (trk // NYH) % NX, trk % NYH
    y_lo, core = grp // NC, grp % NC
    return grp, trk, z, x, y_hi, y_lo, core


def trk_of(z, x, y_hi):
    return (z * NX + x) * NYH + y_hi


def remote(src, dst, send, recv, grp, trk):
    return pltpu.make_async_remote_copy(
        src_ref=src, dst_ref=dst, send_sem=send, recv_sem=recv,
        device_id=(grp, trk), device_id_type=MESH,
    )


def landed(view, recv, grp, trk):
    remote(view, view, recv, recv, grp, trk).wait_recv()


def left(view, send, grp, trk):
    remote(view, view, send, send, grp, trk).wait_send()


def lanes(grp):
    return pl.ds(pl.multiple_of(grp * 128, 128), 128)


def flips(value, count, stride):
    bits = count.bit_length() - 1
    return [(1 - 2 * ((value // 2**b) % 2)) * (2**b * stride) for b in range(bits)]


def row_kernel(
    f_ref, u_ref, w_ref, gain_ref, out_ref, gw_ref, gg_ref,
    fs, us, fr, ur, wf, wt, cen_ref, inv_ref, prob_ref,
    up, nor, qr, kr, vr, gar, atr, gqr, gkr, gvr, branch,
    raw, got_c, acc_c, got_d, acc, got_z,
    sum_c, sum_y, sum_z,
    local, send_a, recv_a, send_w, recv_w, send_g, recv_g, send_s, recv_s,
):
    grp, trk, z, x, y_hi, y_lo, core = position()
    tracks, cells, width = f_ref.shape
    length = tracks * cells
    plane = NX * NYH
    ny = NYL * NYH
    y_at = y_hi * NYL + y_lo
    sibling = y_lo * NC + 1 - core

    def y_peer(s):
        return (y_lo + s % 2) % NYL, (y_hi + s // 2) % NYH

    z_peers = [(grp, trk_of((z + s) % NZ, x, y_hi)) for s in range(1, NZ)]
    x_peers = [(grp, trk_of(z, (x + s) % NX, y_hi)) for s in range(1, NX)]
    y_peers = []
    for s in range(1, ny):
        low, high = y_peer(s)
        y_peers.append((low * NC + core, trk_of(z, x, high)))

    xy_at = y_at * NX + x
    plane_peers = []
    for s in range(ny):
        low, high = y_peer(s)
        for far in range(NX):
            if s + far > 0:
                at_x = (x + far) % NX
                plane_peers.append((low, high, at_x, (low * NC + core, trk_of(z, at_x, high))))

    loads = [
        pltpu.make_async_copy(src, dst, local.at[3 + i])
        for i, (src, dst) in enumerate(((f_ref, fs), (u_ref, us)))
    ]
    for load in loads:
        load.start()
    mine = wf.at[:, z, x, y_hi, :, lanes(grp)]
    own = pltpu.make_async_copy(w_ref, mine, local.at[2])
    own.start()

    barrier = pltpu.get_barrier_semaphore()

    def greet(step, carry):
        to = lax.rem(trk + tracks // 2 + step, tracks)
        pl.semaphore_signal(barrier, inc=1, device_id=(grp, to), device_id_type=MESH)
        return carry

    lax.fori_loop(0, tracks // 2, greet, 0)
    lax.fori_loop(tracks // 2 + 1, tracks, greet, 0)
    for k in range(plane):
        to = ((1 - y_lo) * NC + core, z * plane + k)
        pl.semaphore_signal(barrier, inc=1, device_id=to, device_id_type=MESH)
    pl.semaphore_signal(barrier, inc=1, device_id=(sibling, trk), device_id_type=MESH)
    pl.semaphore_wait(barrier, tracks - 1 + plane + 1)

    for peer in z_peers:
        remote(w_ref, mine, send_w.at[0], recv_w.at[0], *peer).start()
    for load in loads:
        load.wait()

    in_plane = flips(trk % plane, plane, 1)
    over_z = flips(z, NZ, plane)
    offsets = []
    for k in range(plane):
        offset = trk * 0
        for b, flip in enumerate(in_plane):
            if (k >> b) & 1:
                offset = offset + flip
        offsets.append(offset)

    def exchange(src, dst, at, first, last):
        def some(high, skip):
            base = trk
            for b, flip in enumerate(over_z):
                base = base + ((high // 2**b) % 2) * flip
            for k in range(skip, plane):
                to = base + offsets[k]
                remote(src.at[to], dst.at[trk], send_a.at[at], recv_a.at[at], grp, to).start()

        def step(high, carry):
            some(high, 0)
            return carry

        if first == 0:
            pltpu.make_async_copy(src.at[trk], dst.at[trk], local.at[min(at, 1)]).start()
            some(0, 1)
            first = 1
        lax.fori_loop(first, last, step, 0)

    def exchanged(src, dst, at):
        landed(dst.at[: tracks - 1], recv_a.at[at], grp, trk)
        pltpu.make_async_copy(src.at[trk], dst.at[trk], local.at[min(at, 1)]).wait()

    exchange(fs, fr, 0, 0, NZ)
    own.wait()
    landed(wf.at[:, : NZ - 1, 0, 0, :, :128], recv_w.at[0], grp, trk)
    by_x = wf.at[:2, :, x, y_hi, :, lanes(grp)]
    by_y = wf.at[2:, :, x, y_hi, :, lanes(grp)]
    for peer in x_peers:
        remote(by_x, by_x, send_w.at[1], recv_w.at[1], *peer).start()
    for peer in y_peers:
        remote(by_y, by_y, send_w.at[10], recv_w.at[10], *peer).start()
    exchange(us, ur, 1, 0, NZ // 2)
    landed(wf.at[:2, :, : NX - 1, 0, :, :128], recv_w.at[1], grp, trk)
    landed(wf.at[2:, :, 0, 0, :, : (ny - 1) * 128], recv_w.at[10], grp, trk)
    for m in (0, 2, 1, 3):
        if m < 2:
            part = wf.at[m, :, :, y_hi, :, lanes(grp)]
            for peer in y_peers:
                remote(part, part, send_w.at[2 + m], recv_w.at[2 + m], *peer).start()
        else:
            for s in range(ny):
                low, high = y_peer(s)
                part = wf.at[m, :, x, high, :, lanes(low * NC + core)]
                for peer in x_peers:
                    remote(part, part, send_w.at[2 + m], recv_w.at[2 + m], *peer).start()
    exchange(us, ur, 1, NZ // 2, NZ)

    def last_stage(m):
        if m < 2:
            return wf.at[m, :, :, 0, :, : (ny - 1) * 128]
        return wf.at[m, :, : NX - 1, :, :, : ny // NYH * 128]

    def swap_weights(m):
        landed(last_stage(m), recv_w.at[2 + m], grp, trk)
        for low in range(NYL):
            half = wf.at[m, :, :, :, :, lanes(low * NC + core)]
            remote(half, half, send_w.at[6 + m], recv_w.at[6 + m], sibling, trk).start()

    def take_weights(m):
        landed(wf.at[m, :, :, :, :, : NYL * 128], recv_w.at[6 + m], grp, trk)
        wt[m] = wf[m].astype(F32).reshape(width, width).astype(BF16)

    for m in (0, 2, 1, 3):
        swap_weights(m)

    gain = gain_ref[...]
    exchanged(fs, fr, 0)
    values = fr[...].astype(F32).reshape(length, width)
    offset = values - jnp.mean(values, -1, keepdims=True)
    inv_std = lax.rsqrt(jnp.mean(offset * offset, -1, keepdims=True) + 1e-05)
    centred = offset * inv_std
    cen_ref[...] = centred
    inv_ref[...] = inv_std
    nor[...] = (centred * gain).astype(BF16)
    scaling = jnp.asarray(HEAD ** (-0.5), BF16)
    for m, ref in ((0, qr), (2, vr), (1, kr)):
        take_weights(m)
        ref[...] = dot(nor[...], wt[m], 1, 1).astype(BF16)
    half = length // 2
    lane = lax.broadcasted_iota(jnp.int32, (1, 128), 1)
    masks = [((lane >= h * HEAD) & (lane < (h + 1) * HEAD)).astype(BF16) for h in range(2)]
    turned = lax.broadcasted_iota(jnp.int32, (128, 1), 0)
    turned_masks = [
        ((turned >= h * HEAD) & (turned < (h + 1) * HEAD)).astype(BF16) for h in range(2)
    ]
    pairs = width // 128

    def forward(pair, carry):
        cols = lanes(pair)
        q, k, v = qr[:, cols] * scaling, kr[:, cols], vr[:, cols]
        v_turned = v.T
        k_of = [k * masks[h] for h in range(2)]
        v_of = [v_turned * turned_masks[h] for h in range(2)]
        for part in range(2):
            rows = slice(part * half, (part + 1) * half)
            sum_o = jnp.zeros((128, half), F32)
            for h in range(2):
                scores = dot(k_of[h], q[rows], 1, 1)
                shifted = jnp.exp(scores - jnp.max(scores, 0, keepdims=True))
                prob = shifted * (1.0 / jnp.sum(shifted, 0, keepdims=True))
                prob_ref[2 * pair + h, part] = prob
                sum_o += dot(v_of[h], prob.astype(BF16), 1, 0)
            atr[rows, cols] = sum_o.T.astype(BF16)
        return carry

    lax.fori_loop(0, pairs, forward, 0)

    def chunk(c):
        if c == 0:
            return slice(3, 4), slice(0, NZ)
        return slice(0, 3), slice((c - 1) * NZ // pairs, c * NZ // pairs)

    def core_start(c):
        ms, zs = chunk(c)
        for low in range(NYL):
            theirs = raw.at[ms, zs, :, :, :, lanes(low * NC + 1 - core)]
            remote(
                theirs, got_c.at[low, ms, zs], send_g.at[0, c], recv_g.at[0, c], sibling, trk
            ).start()

    def core_finish(c):
        ms, zs = chunk(c)
        landed(got_c.at[:, ms, zs], recv_g.at[0, c], grp, trk)
        for low in range(NYL):
            acc_c[low, ms, zs] = (
                raw[ms, zs, :, :, :, lanes(low * NC + core)].astype(F32)
                + got_c[low, ms, zs].astype(F32)
            ).astype(BF16)
        for low, high, at_x, to in plane_peers:
            remote(
                acc_c.at[low, ms, zs, at_x, high], got_d.at[xy_at, ms, zs],
                send_g.at[1, c], recv_g.at[1, c], *to,
            ).start()

    def plane_finish(c):
        ms, zs = chunk(c)
        landed(got_d.at[: ny * NX - 1, ms, zs], recv_g.at[1, c], grp, trk)
        total = acc_c[y_lo, ms, zs, x, y_hi].astype(F32)
        for low, high, at_x, _ in plane_peers:
            total += got_d[(high * NYL + low) * NX + at_x, ms, zs].astype(F32)
        acc[ms, zs] = total.astype(BF16)

    raw_tiles = raw.shape[2:]

    take_weights(3)
    exchanged(us, ur, 1)
    up[...] = ur[...].astype(F32).reshape(length, width).astype(BF16)
    gar[...] = dot(up[...], wt[3], 1, 0).astype(BF16)
    raw[3] = dot(up[...], atr[...], 0, 0).reshape(raw.shape[1:]).astype(BF16)
    core_start(0)
    for pair in range(pairs):
        cols = slice(pair * 128, (pair + 1) * 128)
        q, k, v, ga = qr[:, cols], kr[:, cols], vr[:, cols], gar[:, cols]
        scaled_ga = ga * scaling
        k_turned = k.T
        k_of = [k_turned * turned_masks[h] for h in range(2)]
        v_of = [v * masks[h] for h in range(2)]
        q_of = [q * masks[h] for h in range(2)]
        ga_of = [ga * masks[h] for h in range(2)]
        sum_k = jnp.zeros((length, 128), F32)
        sum_v = jnp.zeros((length, 128), F32)
        for part in range(2):
            rows = slice(part * half, (part + 1) * half)
            sum_q = jnp.zeros((128, half), F32)
            for h in range(2):
                prob = prob_ref[2 * pair + h, part]
                dprobs = dot(v_of[h], scaled_ga[rows], 1, 1)
                row_dot = jnp.sum(prob * dprobs, 0, keepdims=True)
                grad = (prob * (dprobs - row_dot)).astype(BF16)
                sum_q += dot(k_of[h], grad, 1, 0)
                sum_v += dot(prob.astype(BF16), ga_of[h][rows], 1, 0)
                sum_k += dot(grad, q_of[h][rows], 1, 0)
            gqr[cols, rows] = sum_q.astype(BF16)
        gkr[:, cols] = sum_k.astype(BF16)
        gvr[:, cols] = sum_v.astype(BF16)
        zs = chunk(pair + 1)[1]
        for m, piece in enumerate((
            dot(gqr[cols, :], nor[...], 1, 0),
            dot(gkr[:, cols], nor[...], 0, 0),
            dot(gvr[:, cols], nor[...], 0, 0),
        )):
            raw[m, zs] = piece.reshape((zs.stop - zs.start,) + raw_tiles).astype(BF16)
        core_start(pair + 1)
        core_finish(pair)
    grad_normed = (
        dot(gqr[...], wt[0], 0, 0) + dot(gkr[...], wt[1], 1, 0) + dot(gvr[...], wt[2], 1, 0)
    )
    centred = cen_ref[...]
    sum_c[core] = jnp.sum(grad_normed * centred, 0, keepdims=True)
    remote(sum_c.at[core], sum_c.at[core], send_s.at[0], recv_s.at[0], sibling, trk).start()
    core_finish(pairs)
    scaled = grad_normed * gain
    grad = inv_ref[...] * (
        scaled
        - jnp.mean(scaled, -1, keepdims=True)
        - centred * jnp.mean(scaled * centred, -1, keepdims=True)
    )
    grad = up[...].astype(F32) + grad.astype(BF16).astype(F32)
    branch[...] = grad.reshape(tracks, cells, width).astype(BF16)
    exchange(branch, out_ref, 2, 0, NZ)
    landed(sum_c.at[0], recv_s.at[0], grp, trk)
    sum_y[xy_at] = sum_c[0] + sum_c[1]
    for _, _, _, to in plane_peers:
        remote(sum_y.at[xy_at], sum_y.at[xy_at], send_s.at[1], recv_s.at[1], *to).start()
    for c in range(pairs + 1):
        plane_finish(c)
    for s in range(1, NZ):
        remote(
            acc.at[:, (z + s) % NZ], got_z.at[z], send_g.at[2, 0], recv_g.at[2, 0],
            *z_peers[s - 1],
        ).start()
    landed(sum_y.at[: ny * NX - 1], recv_s.at[1], grp, trk)
    all_y = sum_y[0]
    for s in range(1, ny * NX):
        all_y += sum_y[s]
    sum_z[z] = all_y
    for peer in z_peers:
        remote(sum_z.at[z], sum_z.at[z], send_s.at[2], recv_s.at[2], *peer).start()
    landed(got_z.at[: NZ - 1], recv_g.at[2, 0], grp, trk)
    total = acc[:, z].astype(F32)
    for s in range(1, NZ):
        total += got_z[(z + s) % NZ].astype(F32)
    factor = float(length * lax.axis_size("grp") * tracks) ** (-0.5)
    gw_ref[...] = total * factor
    landed(sum_z.at[: NZ - 1], recv_s.at[2], grp, trk)
    all_z = sum_z[0]
    for s in range(1, NZ):
        all_z += sum_z[s]
    gg_ref[...] = all_z * factor
    exchanged(branch, out_ref, 2)

    for at in range(3):
        left(out_ref.at[: tracks - 1], send_a.at[at], grp, trk)
    left(wf.at[:, : NZ - 1, 0, 0, :, :128], send_w.at[0], grp, trk)
    left(wf.at[:2, :, : NX - 1, 0, :, :128], send_w.at[1], grp, trk)
    left(wf.at[2:, :, 0, 0, :, : (ny - 1) * 128], send_w.at[10], grp, trk)
    for m in range(4):
        left(last_stage(m), send_w.at[2 + m], grp, trk)
        left(wf.at[m, :, :, :, :, : NYL * 128], send_w.at[6 + m], grp, trk)
    for c in range(pairs + 1):
        ms, zs = chunk(c)
        left(got_c.at[:, ms, zs], send_g.at[0, c], grp, trk)
        left(got_d.at[: ny * NX - 1, ms, zs], send_g.at[1, c], grp, trk)
    left(got_z.at[: NZ - 1], send_g.at[2, 0], grp, trk)
    left(sum_c.at[0], send_s.at[0], grp, trk)
    left(sum_y.at[: ny * NX - 1], send_s.at[1], grp, trk)
    left(sum_z.at[: NZ - 1], send_s.at[2], grp, trk)


def layer_back(fields, upstream, w_tile, gain):
    tracks, cells, width = fields.shape
    outs = w_tile.shape[1]
    length = tracks * cells
    ny = NYL * NYH
    any_, vmem = pl.BlockSpec(memory_space=pl.ANY), pl.BlockSpec(memory_space=pltpu.VMEM)
    dma = pltpu.SemaphoreType.DMA
    square = pltpu.VMEM((length, width), BF16)
    row = pltpu.VMEM((tracks, cells, width), BF16)
    return pl.pallas_call(
        row_kernel,
        out_shape=(
            jax.ShapeDtypeStruct((tracks, cells, width), BF16),
            jax.ShapeDtypeStruct((4, outs, 128), F32),
            jax.ShapeDtypeStruct((1, width), F32),
        ),
        in_specs=[any_, any_, any_, vmem],
        out_specs=[any_, vmem, vmem],
        scratch_shapes=[
            row,
            row,
            row,
            row,
            pltpu.VMEM((4, NZ, NX, NYH, outs, width), BF16),
            pltpu.VMEM((4, width, width), BF16),
            pltpu.VMEM((length, width), F32),
            pltpu.VMEM((length, 1), F32),
            pltpu.VMEM((width // HEAD, 2, length, length // 2), F32),
        ]
        + [square] * 7
        + [pltpu.VMEM((width, length), BF16)]
        + [square] * 2
        + [
            row,
            pltpu.VMEM((4, NZ, NX, NYH, outs, width), BF16),
            pltpu.VMEM((NYL, 4, NZ, NX, NYH, outs, 128), BF16),
            pltpu.VMEM((NYL, 4, NZ, NX, NYH, outs, 128), BF16),
            pltpu.VMEM((ny * NX, 4, NZ, outs, 128), BF16),
            pltpu.VMEM((4, NZ, outs, 128), BF16),
            pltpu.VMEM((NZ, 4, outs, 128), BF16),
            pltpu.VMEM((NC, 1, width), F32),
            pltpu.VMEM((ny * NX, 1, width), F32),
            pltpu.VMEM((NZ, 1, width), F32),
            dma((5,)),
            dma((3,)),
            dma((3,)),
            dma((11,)),
            dma((11,)),
            dma((3, 5)),
            dma((3, 5)),
            dma((3,)),
            dma((3,)),
        ],
        compiler_params=pltpu.CompilerParams(
            collective_id=1, has_side_effects=True, vmem_limit_bytes=56 << 20
        ),
        name="layer_back",
    )(fields, upstream, w_tile, gain)


def shards(fields, upstream, ln_gain, weights):
    tracks, cells, width = fields.shape
    w_tile = jnp.swapaxes(weights, 1, 2)
    grad_fields, grad_tile, grad_gain = layer_back(
        fields, upstream, w_tile, ln_gain.reshape(1, width)
    )
    return grad_fields, jnp.swapaxes(grad_tile, 1, 2), grad_gain.reshape(width)


def solution(mesh):
    in_specs = (P("grp", "trk", None), P("grp", "trk", None), P(), P(None, "grp", "trk"))
    out_specs = (P("grp", "trk", None), P(None, "grp", "trk"), P())
    return jax.shard_map(shards, mesh=mesh, in_specs=in_specs, out_specs=out_specs, check_vma=False)
```

```python
import jax
import jax.numpy as jnp
from jax import lax
from jax.experimental import pallas as pl
from jax.experimental.pallas import tpu as pltpu
from jax.sharding import PartitionSpec as P

NZ, NX, NYH = 8, 4, 2
NYL, NC = 2, 2
HEAD = 64
MESH = pl.DeviceIdType.MESH
F32, BF16 = jnp.float32, jnp.bfloat16


def dot(a, b, ca, cb):
    return lax.dot_general(a, b, (((ca,), (cb,)), ((), ())), preferred_element_type=F32)


def position():
    grp, trk = lax.axis_index("grp"), lax.axis_index("trk")
    z, x, y_hi = trk // (NX * NYH), (trk // NYH) % NX, trk % NYH
    y_lo, core = grp // NC, grp % NC
    return grp, trk, z, x, y_hi, y_lo, core


def trk_of(z, x, y_hi):
    return (z * NX + x) * NYH + y_hi


def remote(src, dst, send, recv, grp, trk):
    return pltpu.make_async_remote_copy(
        src_ref=src, dst_ref=dst, send_sem=send, recv_sem=recv,
        device_id=(grp, trk), device_id_type=MESH,
    )


def landed(view, recv, grp, trk):
    remote(view, view, recv, recv, grp, trk).wait_recv()


def left(view, send, grp, trk):
    remote(view, view, send, send, grp, trk).wait_send()


def lanes(grp):
    return pl.ds(pl.multiple_of(grp * 128, 128), 128)


def flips(value, count, stride):
    bits = count.bit_length() - 1
    return [(1 - 2 * ((value // 2**b) % 2)) * (2**b * stride) for b in range(bits)]


def row_kernel(
    f_ref, u_ref, w_ref, gain_ref, out_ref, gw_ref, gg_ref,
    fs, us, fr, ur, wf, wt, cen_ref, inv_ref, prob_ref,
    up, nor, qr, kr, vr, gar, atr, gqr, gkr, gvr, branch,
    raw, got_c, acc_c, got_y, acc_y, got_x, got_xf, acc_xf, got_yl, got_d, acc, got_z,
    sum_c, sum_y, sum_z,
    local, send_a, recv_a, send_w, recv_w, send_g, recv_g, send_s, recv_s,
):
    grp, trk, z, x, y_hi, y_lo, core = position()
    tracks, cells, width = f_ref.shape
    length = tracks * cells
    plane = NX * NYH
    ny = NYL * NYH
    y_at = y_hi * NYL + y_lo
    sibling = y_lo * NC + 1 - core

    def y_peer(s):
        return (y_lo + s % 2) % NYL, (y_hi + s // 2) % NYH

    z_peers = [(grp, trk_of((z + s) % NZ, x, y_hi)) for s in range(1, NZ)]
    x_peers = [(grp, trk_of(z, (x + s) % NX, y_hi)) for s in range(1, NX)]
    y_peers = []
    for s in range(1, ny):
        low, high = y_peer(s)
        y_peers.append((low * NC + core, trk_of(z, x, high)))

    xy_at = y_at * NX + x
    plane_peers = []
    for s in range(ny):
        low, high = y_peer(s)
        for far in range(NX):
            if s + far > 0:
                at_x = (x + far) % NX
                plane_peers.append((low, high, at_x, (low * NC + core, trk_of(z, at_x, high))))

    loads = [
        pltpu.make_async_copy(src, dst, local.at[3 + i])
        for i, (src, dst) in enumerate(((f_ref, fs), (u_ref, us)))
    ]
    for load in loads:
        load.start()
    mine = wf.at[:, z, x, y_hi, :, lanes(grp)]
    own = pltpu.make_async_copy(w_ref, mine, local.at[2])
    own.start()

    barrier = pltpu.get_barrier_semaphore()

    def greet(step, carry):
        to = lax.rem(trk + tracks // 2 + step, tracks)
        pl.semaphore_signal(barrier, inc=1, device_id=(grp, to), device_id_type=MESH)
        return carry

    lax.fori_loop(0, tracks // 2, greet, 0)
    lax.fori_loop(tracks // 2 + 1, tracks, greet, 0)
    for k in range(plane):
        to = ((1 - y_lo) * NC + core, z * plane + k)
        pl.semaphore_signal(barrier, inc=1, device_id=to, device_id_type=MESH)
    pl.semaphore_signal(barrier, inc=1, device_id=(sibling, trk), device_id_type=MESH)
    pl.semaphore_wait(barrier, tracks - 1 + plane + 1)

    for peer in z_peers:
        remote(w_ref, mine, send_w.at[0], recv_w.at[0], *peer).start()
    for load in loads:
        load.wait()

    in_plane = flips(trk % plane, plane, 1)
    over_z = flips(z, NZ, plane)
    offsets = []
    for k in range(plane):
        offset = trk * 0
        for b, flip in enumerate(in_plane):
            if (k >> b) & 1:
                offset = offset + flip
        offsets.append(offset)

    def exchange(src, dst, at, first, last):
        def some(high, skip):
            base = trk
            for b, flip in enumerate(over_z):
                base = base + ((high // 2**b) % 2) * flip
            for k in range(skip, plane):
                to = base + offsets[k]
                remote(src.at[to], dst.at[trk], send_a.at[at], recv_a.at[at], grp, to).start()

        def step(high, carry):
            some(high, 0)
            return carry

        if first == 0:
            pltpu.make_async_copy(src.at[trk], dst.at[trk], local.at[min(at, 1)]).start()
            some(0, 1)
            first = 1
        lax.fori_loop(first, last, step, 0)

    def exchanged(src, dst, at):
        landed(dst.at[: tracks - 1], recv_a.at[at], grp, trk)
        pltpu.make_async_copy(src.at[trk], dst.at[trk], local.at[min(at, 1)]).wait()

    exchange(fs, fr, 0, 0, NZ)
    exchange(us, ur, 1, 0, NZ)
    own.wait()
    landed(wf.at[:, : NZ - 1, 0, 0, :, :128], recv_w.at[0], grp, trk)
    by_x = wf.at[:2, :, x, y_hi, :, lanes(grp)]
    by_y = wf.at[2:, :, x, y_hi, :, lanes(grp)]
    for peer in x_peers:
        remote(by_x, by_x, send_w.at[1], recv_w.at[1], *peer).start()
    for peer in y_peers:
        remote(by_y, by_y, send_w.at[10], recv_w.at[10], *peer).start()
    landed(wf.at[:2, :, : NX - 1, 0, :, :128], recv_w.at[1], grp, trk)
    landed(wf.at[2:, :, 0, 0, :, : (ny - 1) * 128], recv_w.at[10], grp, trk)
    for m in (0, 2, 1, 3):
        if m < 2:
            part = wf.at[m, :, :, y_hi, :, lanes(grp)]
            for peer in y_peers:
                remote(part, part, send_w.at[2 + m], recv_w.at[2 + m], *peer).start()
        else:
            for s in range(ny):
                low, high = y_peer(s)
                part = wf.at[m, :, x, high, :, lanes(low * NC + core)]
                for peer in x_peers:
                    remote(part, part, send_w.at[2 + m], recv_w.at[2 + m], *peer).start()

    def last_stage(m):
        if m < 2:
            return wf.at[m, :, :, 0, :, : (ny - 1) * 128]
        return wf.at[m, :, : NX - 1, :, :, : ny // NYH * 128]

    def swap_weights(m):
        landed(last_stage(m), recv_w.at[2 + m], grp, trk)
        for low in range(NYL):
            half = wf.at[m, :, :, :, :, lanes(low * NC + core)]
            remote(half, half, send_w.at[6 + m], recv_w.at[6 + m], sibling, trk).start()

    def take_weights(m):
        landed(wf.at[m, :, :, :, :, : NYL * 128], recv_w.at[6 + m], grp, trk)
        wt[m] = wf[m].astype(F32).reshape(width, width).astype(BF16)

    for m in (0, 2, 1, 3):
        swap_weights(m)

    gain = gain_ref[...]
    exchanged(fs, fr, 0)
    values = fr[...].astype(F32).reshape(length, width)
    offset = values - jnp.mean(values, -1, keepdims=True)
    inv_std = lax.rsqrt(jnp.mean(offset * offset, -1, keepdims=True) + 1e-05)
    centred = offset * inv_std
    cen_ref[...] = centred
    inv_ref[...] = inv_std
    nor[...] = (centred * gain).astype(BF16)
    scaling = jnp.asarray(HEAD ** (-0.5), BF16)
    for m, ref in ((0, qr), (2, vr), (1, kr)):
        take_weights(m)
        ref[...] = dot(nor[...], wt[m], 1, 1).astype(BF16)
    half = length // 2
    lane = lax.broadcasted_iota(jnp.int32, (1, 128), 1)
    masks = [((lane >= h * HEAD) & (lane < (h + 1) * HEAD)).astype(BF16) for h in range(2)]
    turned = lax.broadcasted_iota(jnp.int32, (128, 1), 0)
    turned_masks = [
        ((turned >= h * HEAD) & (turned < (h + 1) * HEAD)).astype(BF16) for h in range(2)
    ]
    pairs = width // 128

    def forward(pair, carry):
        cols = lanes(pair)
        q, k, v = qr[:, cols] * scaling, kr[:, cols], vr[:, cols]
        v_turned = v.T
        k_of = [k * masks[h] for h in range(2)]
        v_of = [v_turned * turned_masks[h] for h in range(2)]
        for part in range(2):
            rows = slice(part * half, (part + 1) * half)
            sum_o = jnp.zeros((128, half), F32)
            for h in range(2):
                scores = dot(k_of[h], q[rows], 1, 1)
                shifted = jnp.exp(scores - jnp.max(scores, 0, keepdims=True))
                prob = shifted * (1.0 / jnp.sum(shifted, 0, keepdims=True))
                prob_ref[2 * pair + h, part] = prob
                sum_o += dot(v_of[h], prob.astype(BF16), 1, 0)
            atr[rows, cols] = sum_o.T.astype(BF16)
        return carry

    lax.fori_loop(0, pairs, forward, 0)

    def chunk(c):
        if c == 0:
            return slice(3, 4), slice(0, NZ)
        return slice(0, 3), slice((c - 1) * NZ // pairs, c * NZ // pairs)

    def y_first(c):
        return c > 0, slice(0, 2), chunk(c)[1]

    def x_first(c):
        return slice(2, 3) if c > 0 else slice(3, 4), chunk(c)[1]

    def core_start(c):
        ms, zs = chunk(c)
        for low in range(NYL):
            theirs = raw.at[ms, zs, :, :, :, lanes(low * NC + 1 - core)]
            remote(
                theirs, got_c.at[low, ms, zs], send_g.at[0, c], recv_g.at[0, c], sibling, trk
            ).start()

    def core_finish(c):
        ms, zs = chunk(c)
        landed(got_c.at[:, ms, zs], recv_g.at[0, c], grp, trk)
        for low in range(NYL):
            acc_c[low, ms, zs] = (
                raw[ms, zs, :, :, :, lanes(low * NC + core)].astype(F32)
                + got_c[low, ms, zs].astype(F32)
            ).astype(BF16)
        if c == pairs:
            for low, high, at_x, to in plane_peers:
                remote(
                    acc_c.at[low, ms, zs, at_x, high], got_d.at[xy_at],
                    send_g.at[1, c], recv_g.at[1, c], *to,
                ).start()
            return
        there, ms, zs = y_first(c)
        if there:
            for s in range(1, ny):
                low, high = y_peer(s)
                remote(
                    acc_c.at[low, ms, zs, :, high], got_y.at[y_at, ms, zs],
                    send_g.at[1, c], recv_g.at[1, c], *y_peers[s - 1],
                ).start()
        ms, zs = x_first(c)
        for s in range(1, NX):
            remote(
                acc_c.at[:, ms, zs, (x + s) % NX], got_xf.at[x, :, ms, zs],
                send_g.at[2, c], recv_g.at[2, c], *x_peers[s - 1],
            ).start()

    def second_start(c):
        there, ms, zs = y_first(c)
        if there:
            landed(got_y.at[: ny - 1, ms, zs], recv_g.at[1, c], grp, trk)
            total = acc_c[y_lo, ms, zs, :, y_hi].astype(F32)
            for s in range(1, ny):
                low, high = y_peer(s)
                total += got_y[high * NYL + low, ms, zs].astype(F32)
            acc_y[ms, zs] = total.astype(BF16)
            for s in range(1, NX):
                remote(
                    acc_y.at[ms, zs, (x + s) % NX], got_x.at[x, ms, zs],
                    send_g.at[3, c], recv_g.at[3, c], *x_peers[s - 1],
                ).start()
        ms, zs = x_first(c)
        landed(got_xf.at[: NX - 1, :, ms, zs], recv_g.at[2, c], grp, trk)
        total = acc_c[:, ms, zs, x].astype(F32)
        for s in range(1, NX):
            total += got_xf[(x + s) % NX, :, ms, zs].astype(F32)
        acc_xf[:, ms, zs] = total.astype(BF16)
        for s in range(1, ny):
            low, high = y_peer(s)
            remote(
                acc_xf.at[low, ms, zs, high], got_yl.at[y_at, ms, zs],
                send_g.at[4, c], recv_g.at[4, c], *y_peers[s - 1],
            ).start()

    def direct_finish(c):
        ms, zs = chunk(c)
        landed(got_d.at[: ny * NX - 1], recv_g.at[1, c], grp, trk)
        total = acc_c[y_lo, ms, zs, x, y_hi].astype(F32)
        for low, high, at_x, _ in plane_peers:
            total += got_d[(high * NYL + low) * NX + at_x].astype(F32)
        acc[ms, zs] = total.astype(BF16)

    def second_finish(c):
        there, ms, zs = y_first(c)
        if there:
            landed(got_x.at[: NX - 1, ms, zs], recv_g.at[3, c], grp, trk)
            total = acc_y[ms, zs, x].astype(F32)
            for s in range(1, NX):
                total += got_x[(x + s) % NX, ms, zs].astype(F32)
            acc[ms, zs] = total.astype(BF16)
        ms, zs = x_first(c)
        landed(got_yl.at[: ny - 1, ms, zs], recv_g.at[4, c], grp, trk)
        total = acc_xf[y_lo, ms, zs, y_hi].astype(F32)
        for s in range(1, ny):
            low, high = y_peer(s)
            total += got_yl[high * NYL + low, ms, zs].astype(F32)
        acc[ms, zs] = total.astype(BF16)

    raw_tiles = raw.shape[2:]

    take_weights(3)
    exchanged(us, ur, 1)
    up[...] = ur[...].astype(F32).reshape(length, width).astype(BF16)
    gar[...] = dot(up[...], wt[3], 1, 0).astype(BF16)
    raw[3] = dot(up[...], atr[...], 0, 0).reshape(raw.shape[1:]).astype(BF16)
    core_start(0)
    for pair in range(pairs):
        cols = slice(pair * 128, (pair + 1) * 128)
        q, k, v, ga = qr[:, cols], kr[:, cols], vr[:, cols], gar[:, cols]
        scaled_ga = ga * scaling
        k_turned = k.T
        k_of = [k_turned * turned_masks[h] for h in range(2)]
        v_of = [v * masks[h] for h in range(2)]
        q_of = [q * masks[h] for h in range(2)]
        ga_of = [ga * masks[h] for h in range(2)]
        sum_k = jnp.zeros((length, 128), F32)
        sum_v = jnp.zeros((length, 128), F32)
        for part in range(2):
            rows = slice(part * half, (part + 1) * half)
            sum_q = jnp.zeros((128, half), F32)
            for h in range(2):
                prob = prob_ref[2 * pair + h, part]
                dprobs = dot(v_of[h], scaled_ga[rows], 1, 1)
                row_dot = jnp.sum(prob * dprobs, 0, keepdims=True)
                grad = (prob * (dprobs - row_dot)).astype(BF16)
                sum_q += dot(k_of[h], grad, 1, 0)
                sum_v += dot(prob.astype(BF16), ga_of[h][rows], 1, 0)
                sum_k += dot(grad, q_of[h][rows], 1, 0)
            gqr[cols, rows] = sum_q.astype(BF16)
        gkr[:, cols] = sum_k.astype(BF16)
        gvr[:, cols] = sum_v.astype(BF16)
        zs = chunk(pair + 1)[1]
        for m, piece in enumerate((
            dot(gqr[cols, :], nor[...], 1, 0),
            dot(gkr[:, cols], nor[...], 0, 0),
            dot(gvr[:, cols], nor[...], 0, 0),
        )):
            raw[m, zs] = piece.reshape((zs.stop - zs.start,) + raw_tiles).astype(BF16)
        core_start(pair + 1)
        core_finish(pair)
    grad_normed = (
        dot(gqr[...], wt[0], 0, 0) + dot(gkr[...], wt[1], 1, 0) + dot(gvr[...], wt[2], 1, 0)
    )
    centred = cen_ref[...]
    sum_c[core] = jnp.sum(grad_normed * centred, 0, keepdims=True)
    remote(sum_c.at[core], sum_c.at[core], send_s.at[0], recv_s.at[0], sibling, trk).start()
    core_finish(pairs)
    scaled = grad_normed * gain
    grad = inv_ref[...] * (
        scaled
        - jnp.mean(scaled, -1, keepdims=True)
        - centred * jnp.mean(scaled * centred, -1, keepdims=True)
    )
    grad = up[...].astype(F32) + grad.astype(BF16).astype(F32)
    branch[...] = grad.reshape(tracks, cells, width).astype(BF16)
    exchange(branch, out_ref, 2, 0, NZ)
    landed(sum_c.at[0], recv_s.at[0], grp, trk)
    sum_y[xy_at] = sum_c[0] + sum_c[1]
    for _, _, _, to in plane_peers:
        remote(sum_y.at[xy_at], sum_y.at[xy_at], send_s.at[1], recv_s.at[1], *to).start()
    for c in range(pairs):
        second_start(c)
    direct_finish(pairs)
    for c in range(pairs):
        second_finish(c)
    for s in range(1, NZ):
        remote(
            acc.at[:, (z + s) % NZ], got_z.at[z], send_g.at[5, 0], recv_g.at[5, 0],
            *z_peers[s - 1],
        ).start()
    landed(sum_y.at[: ny * NX - 1], recv_s.at[1], grp, trk)
    all_y = sum_y[0]
    for s in range(1, ny * NX):
        all_y += sum_y[s]
    sum_z[z] = all_y
    for peer in z_peers:
        remote(sum_z.at[z], sum_z.at[z], send_s.at[3], recv_s.at[3], *peer).start()
    landed(got_z.at[: NZ - 1], recv_g.at[5, 0], grp, trk)
    total = acc[:, z].astype(F32)
    for s in range(1, NZ):
        total += got_z[(z + s) % NZ].astype(F32)
    factor = float(length * lax.axis_size("grp") * tracks) ** (-0.5)
    gw_ref[...] = total * factor
    landed(sum_z.at[: NZ - 1], recv_s.at[3], grp, trk)
    all_z = sum_z[0]
    for s in range(1, NZ):
        all_z += sum_z[s]
    gg_ref[...] = all_z * factor
    exchanged(branch, out_ref, 2)

    for at in range(3):
        left(out_ref.at[: tracks - 1], send_a.at[at], grp, trk)
    left(wf.at[:, : NZ - 1, 0, 0, :, :128], send_w.at[0], grp, trk)
    left(wf.at[:2, :, : NX - 1, 0, :, :128], send_w.at[1], grp, trk)
    left(wf.at[2:, :, 0, 0, :, : (ny - 1) * 128], send_w.at[10], grp, trk)
    for m in range(4):
        left(last_stage(m), send_w.at[2 + m], grp, trk)
        left(wf.at[m, :, :, :, :, : NYL * 128], send_w.at[6 + m], grp, trk)
    for c in range(pairs + 1):
        ms, zs = chunk(c)
        left(got_c.at[:, ms, zs], send_g.at[0, c], grp, trk)
        if c == pairs:
            left(got_d.at[: ny * NX - 1], send_g.at[1, c], grp, trk)
            break
        there, ms, zs = y_first(c)
        if there:
            left(got_y.at[: ny - 1, ms, zs], send_g.at[1, c], grp, trk)
            left(got_x.at[: NX - 1, ms, zs], send_g.at[3, c], grp, trk)
        ms, zs = x_first(c)
        left(got_xf.at[: NX - 1, :, ms, zs], send_g.at[2, c], grp, trk)
        left(got_yl.at[: ny - 1, ms, zs], send_g.at[4, c], grp, trk)
    left(got_z.at[: NZ - 1], send_g.at[5, 0], grp, trk)
    left(sum_c.at[0], send_s.at[0], grp, trk)
    left(sum_y.at[: ny * NX - 1], send_s.at[1], grp, trk)
    left(sum_z.at[: NZ - 1], send_s.at[3], grp, trk)


def layer_back(fields, upstream, w_tile, gain):
    tracks, cells, width = fields.shape
    outs = w_tile.shape[1]
    length = tracks * cells
    ny = NYL * NYH
    any_, vmem = pl.BlockSpec(memory_space=pl.ANY), pl.BlockSpec(memory_space=pltpu.VMEM)
    dma = pltpu.SemaphoreType.DMA
    square = pltpu.VMEM((length, width), BF16)
    row = pltpu.VMEM((tracks, cells, width), BF16)
    return pl.pallas_call(
        row_kernel,
        out_shape=(
            jax.ShapeDtypeStruct((tracks, cells, width), BF16),
            jax.ShapeDtypeStruct((4, outs, 128), F32),
            jax.ShapeDtypeStruct((1, width), F32),
        ),
        in_specs=[any_, any_, any_, vmem],
        out_specs=[any_, vmem, vmem],
        scratch_shapes=[
            row,
            row,
            row,
            row,
            pltpu.VMEM((4, NZ, NX, NYH, outs, width), BF16),
            pltpu.VMEM((4, width, width), BF16),
            pltpu.VMEM((length, width), F32),
            pltpu.VMEM((length, 1), F32),
            pltpu.VMEM((width // HEAD, 2, length, length // 2), F32),
        ]
        + [square] * 7
        + [pltpu.VMEM((width, length), BF16)]
        + [square] * 2
        + [
            row,
            pltpu.VMEM((4, NZ, NX, NYH, outs, width), BF16),
            pltpu.VMEM((NYL, 4, NZ, NX, NYH, outs, 128), BF16),
            pltpu.VMEM((NYL, 4, NZ, NX, NYH, outs, 128), BF16),
            pltpu.VMEM((ny, 4, NZ, NX, outs, 128), BF16),
            pltpu.VMEM((4, NZ, NX, outs, 128), BF16),
            pltpu.VMEM((NX, 4, NZ, outs, 128), BF16),
            pltpu.VMEM((NX, NYL, 4, NZ, NYH, outs, 128), BF16),
            pltpu.VMEM((NYL, 4, NZ, NYH, outs, 128), BF16),
            pltpu.VMEM((ny, 4, NZ, outs, 128), BF16),
            pltpu.VMEM((ny * NX, 3, NZ * 128 // width, outs, 128), BF16),
            pltpu.VMEM((4, NZ, outs, 128), BF16),
            pltpu.VMEM((NZ, 4, outs, 128), BF16),
            pltpu.VMEM((NC, 1, width), F32),
            pltpu.VMEM((ny * NX, 1, width), F32),
            pltpu.VMEM((NZ, 1, width), F32),
            dma((5,)),
            dma((3,)),
            dma((3,)),
            dma((11,)),
            dma((11,)),
            dma((6, 5)),
            dma((6, 5)),
            dma((4,)),
            dma((4,)),
        ],
        compiler_params=pltpu.CompilerParams(
            collective_id=1, has_side_effects=True, vmem_limit_bytes=56 << 20
        ),
        name="layer_back",
    )(fields, upstream, w_tile, gain)


def shards(fields, upstream, ln_gain, weights):
    tracks, cells, width = fields.shape
    w_tile = jnp.swapaxes(weights, 1, 2)
    grad_fields, grad_tile, grad_gain = layer_back(
        fields, upstream, w_tile, ln_gain.reshape(1, width)
    )
    return grad_fields, jnp.swapaxes(grad_tile, 1, 2), grad_gain.reshape(width)


def solution(mesh):
    in_specs = (P("grp", "trk", None), P("grp", "trk", None), P(), P(None, "grp", "trk"))
    out_specs = (P("grp", "trk", None), P(None, "grp", "trk"), P())
    return jax.shard_map(shards, mesh=mesh, in_specs=in_specs, out_specs=out_specs, check_vma=False)
```
